32 devices in a mesh: groups: 2 (over y), panels: 4 (over z), cols: 2 (over x), phase: 2 (over core).
Axes of the slice: x: 2, y: 2, z: 4, core: 2. Of those that a mesh axis runs over, the one named last changes fastest.
Arguments:
- base_points: float32 [3, 512], P(None, ('groups', 'panels', 'cols')), parts along dimension 1, may hold values from -6 to 6
- control_points: float32 [3, 2048], replicated, may hold values from -6 to 6
- morph_weights: float32 [4, 3, 2048], P('groups'), parts along dimension 0, may hold values from -0.15 to 0.15
- connectivity: int32 [3, 1024], P(None, ('groups', 'panels', 'cols')), parts along dimension 1, may hold values from 0 to 255, as said below
- free_flags: int32 [1024], P(('groups', 'panels', 'cols')), parts along dimension 0, may hold values 0 or 1
- station_owner: int32 [1024, 1], P(('groups', 'panels', 'cols')), parts along dimension 0, may hold values from 0 to 7; in each aligned block of 64 rows (0 to 63, 64 to 127, ...) at most 20 rows name the same one
- variant_order: int32 [4], P('groups'), parts along dimension 0, may hold values from 0 to 1, each once
- load_velocity: float32 [64, 3], replicated, may hold values from -5 to 5
Outputs:
- shear: float32 [4, 64, 1024], P(('groups', 'phase'), None, ('panels', 'cols')), parts along dimension 0
- moment: float32 [4, 64, 1024], P(('groups', 'phase'), None, ('panels', 'cols')), parts along dimension 0
The draws below stay inside these ranges and needn't reach their ends.
There are 2 independent parts, one for each index of `groups`. The reference program is written for one: setup_inputs(seed, part) draws one part's arguments, and reference() takes and returns one part's arrays. A program takes and returns all parts, laid end to end along the dimension named above; an argument that names none is the same for every part. Nothing has to cross between parts.
Inputs may be any that keep to these rules, and one draw needn't show every extreme that they name: `connectivity`: the vertices of panel i lie in block i // 64 of 32 consecutive vertices: from (i // 64) * 32 to (i // 64 + 1) * 32 - 1. `station_owner`: among the panels of one device (aligned blocks of 64 panels) no station owner is named more than 20 times. `variant_order`: each variant appears once.
All inputs are finite; a program needn't handle non-finite values. No bound on the sum of `free_flags` on one device may be relied on, other than what follows from the above.
Results may differ from the reference program's by a relative error of at most 0.0015.
Values may be sent and summed in bfloat16 or wider, within the bound.
A program may use at most 64 MiB of HBM per device.

```python
import math
import jax
import jax.numpy as jnp
import numpy as np
from jax import lax

PAN_DEV = 64
CONTROL = 2048
LOADS = 64
STATIONS = 128
VERT_DEV = 32
PANELS = 512
VERTS = 256
VARIANTS = 2
STATIONS_ALL = 1024
CAPACITY = 20
N_PANELS = 4
N_COLS = 2


def draw_connectivity(key, part):
    local_rows = jax.random.randint(key, (3, PANELS), 0, VERT_DEV, dtype=jnp.int32)
    block_start = jnp.arange(PANELS, dtype=jnp.int32) // PAN_DEV * VERT_DEV
    return (local_rows + block_start[None, :]).astype(jnp.int32)


def plant(array, own_key, low, largest):
    spot = [jax.random.randint(jax.random.fold_in(own_key, axis), (), 0, length) for axis, length in enumerate(array.shape)]
    longest = array.shape.index(max(array.shape))
    beside = spot[:longest] + [(spot[longest] + 1) % array.shape[longest]] + spot[longest + 1:]
    return array.at[tuple(spot)].set(low).at[tuple(beside)].set(largest)


def levels(rng, extent, split, least, largest):
    factor_of, own = 1.0, jax.random.fold_in(rng, 6)
    for axis_at, shards_of in split:
        steps = jnp.exp(jax.random.uniform(jax.random.fold_in(own, axis_at), (shards_of,), jnp.float32, least / len(split), largest / len(split)))
        factor_of = factor_of * jnp.repeat(steps, extent[axis_at] // shards_of).reshape([-1 if axis == axis_at else 1 for axis in range(len(extent))])
    return factor_of


def routed_block(own_key, own, number, rows, number_of, top, reach, skew):
    ranking = jax.random.permutation(own_key, number_of)
    crowded, common = shares(number_of, rows * top, reach, skew, True), shares(number_of, rows * top, reach, skew, False)
    places = jnp.arange(number_of)

    def named(sizes, rotation):
        used = int((sizes > 0).sum())
        fixed = max(1, used // 4)
        shifted = fixed + (places - fixed + rotation * (used - fixed)) % max(1, number_of - fixed)
        return jnp.zeros((number_of,), jnp.int32).at[ranking[jnp.where(places < fixed, places, shifted)]].set(jnp.asarray(sizes, jnp.int32))

    sizes = jnp.where(number % 4 == 0, named(crowded, number // 4), named(common, number - number // 4 - 1))
    mixed = jax.random.permutation(jax.random.fold_in(own, 3), number_of)
    source_of, taker = mixed[0:number_of // 2 * 2:2], mixed[1:number_of // 2 * 2:2]
    margin = jnp.minimum(sizes[source_of] - 1, reach - sizes[taker]) // 2
    margin = jnp.where((source_of == ranking[0]) | (taker == ranking[0]) | (sizes[taker] == 0), 0, jnp.maximum(margin, 0))
    shifted = jax.random.randint(jax.random.fold_in(own, 4), (number_of // 2,), 0, 1 << 20) % (margin + 1)
    sizes = sizes.at[source_of].add(-shifted).at[taker].add(shifted)
    members = jnp.searchsorted(jnp.cumsum(sizes), jnp.arange(rows * top), side="right").astype(jnp.int32)
    grid = members.reshape(top, rows).T
    grid = grid[jax.random.permutation(jax.random.fold_in(own, 1), rows)]
    rotation = jax.random.randint(jax.random.fold_in(own, 2), (rows, 1), 0, top)
    return jnp.take_along_axis(grid, (jnp.arange(top)[None, :] + rotation) % top, axis=1)


def shares(count, total, bound, slope, full):
    weights = [(1 << 20) // math.isqrt(rank ** slope) + 1 for rank in range(1, count + 1)]
    largest = bound if full else min(bound, max(-(-total // count), total * weights[0] // sum(weights)))
    least = 1 if total - largest >= count - 1 else 0
    given, rest = [largest] + [least] * (count - 1), total - largest - least * (count - 1)
    while rest > 0:
        movable = [i for i in range(1, count) if given[i] < largest] or [i for i in range(1, count) if given[i] < bound]
        whole, budget = sum([weights[i] for i in movable]), rest
        for i in movable:
            more = min(bound - given[i], max(1, budget * weights[i] // whole), rest)
            given[i] = given[i] + more
            rest = rest - more
    return np.array(given)


def noise(stream_key, dims, spread, limit, shards=(), kind=jnp.bfloat16):
    factor_of = levels(stream_key, dims, shards, -0.22, 0.18) if shards else 1.0
    values = jax.random.normal(stream_key, dims, jnp.float32) * spread * factor_of
    return jnp.minimum(jnp.maximum(values, -limit), limit).astype(kind)


def setup_inputs(seed: int = 0, part: int = 0) -> dict:
    streams_of = jax.random.split(jax.random.key(seed), 9)
    part_keys = jax.random.split(jax.random.fold_in(streams_of[8], part), 9)
    base_points = noise(part_keys[0], (3, VERTS), 1.0, 6.0, ((1, 8),), jnp.float32)
    control_points = noise(streams_of[1], (3, CONTROL), 1.0, 6.0, (), jnp.float32)
    morph_weights = noise(part_keys[2], (VARIANTS, 3, CONTROL), 0.025, 0.15, (), jnp.float32)
    connectivity = draw_connectivity(jax.random.fold_in(jax.random.fold_in(streams_of[8], part), 71), part)
    free_flags = plant((jax.random.randint(part_keys[4], (PANELS,), 0, 4) < 1).astype(jnp.int32), jax.random.fold_in(part_keys[4], 1), 0, 1)
    station_owner_keys = jax.random.split(jax.random.fold_in(part_keys[5], 1), PANELS // PAN_DEV)
    station_owner_turns = jax.random.permutation(jax.random.fold_in(part_keys[5], 3), PANELS // PAN_DEV)
    station_owner = jax.vmap(lambda own, number: routed_block(jax.random.fold_in(part_keys[5], 2), own, number, PAN_DEV, N_PANELS * N_COLS, 1, CAPACITY, 2))(station_owner_keys, station_owner_turns).reshape((PANELS, 1))
    variant_order = jax.random.permutation(part_keys[6], VARIANTS).astype(jnp.int32)
    load_velocity = noise(streams_of[7], (LOADS, 3), 1.0, 5.0, (), jnp.float32)
    return dict(base_points=base_points, control_points=control_points, morph_weights=morph_weights, connectivity=connectivity, free_flags=free_flags, station_owner=station_owner, variant_order=variant_order, load_velocity=load_velocity)


HIGH = lax.Precision.HIGHEST
CORE_SQUARE = 0.0025
SKIN_SQUARE = 0.01

def panel_shape(moved_points, corner_rows):
    first_corner = jnp.take(moved_points, corner_rows[0], axis=2)
    second_corner = jnp.take(moved_points, corner_rows[1], axis=2)
    third_corner = jnp.take(moved_points, corner_rows[2], axis=2)
    centroid = (first_corner + second_corner + third_corner) / 3.0
    edge_one = second_corner - first_corner
    edge_two = third_corner - first_corner
    cross_x = edge_one[:, 1] * edge_two[:, 2] - edge_one[:, 2] * edge_two[:, 1]
    cross_y = edge_one[:, 2] * edge_two[:, 0] - edge_one[:, 0] * edge_two[:, 2]
    cross_z = edge_one[:, 0] * edge_two[:, 1] - edge_one[:, 1] * edge_two[:, 0]
    area = 0.5 * jnp.stack([cross_x, cross_y, cross_z], axis=1)
    weight = jnp.sqrt(lax.optimization_barrier(jnp.sum(area * area, axis=1)) + SKIN_SQUARE)
    return (centroid, area, weight)

def apply_influence(centroid, weight, strengths, kernel_scale):

    def per_variant(operands):
        centres, weights, values = operands
        values_wide = values.astype(jnp.float32)
        row_blocks = centres.reshape(3, -1, PAN_DEV).transpose(1, 0, 2)

        def per_block(targets):
            distance = (targets[0][:, None] - centres[0][None, :]) ** 2 + (targets[1][:, None] - centres[1][None, :]) ** 2 + (targets[2][:, None] - centres[2][None, :]) ** 2
            influence = (weights[None, :] * kernel_scale * lax.rsqrt(distance + CORE_SQUARE)).astype(jnp.bfloat16)
            return jnp.dot(values_wide, influence.astype(jnp.float32).T, precision=HIGH)
        result = lax.map(per_block, row_blocks)
        return result.transpose(1, 0, 2).reshape(values.shape[0], -1)
    return lax.map(per_variant, (centroid, weight, strengths))

def reference(base_points, control_points, morph_weights, connectivity, free_flags, station_owner, variant_order, load_velocity):
    chosen = morph_weights[variant_order]
    vertex_blocks = base_points.reshape(3, -1, VERT_DEV).transpose(1, 0, 2)

    def move_block(block_points):
        distance = (control_points[0][:, None] - block_points[0][None, :]) ** 2 + (control_points[1][:, None] - block_points[1][None, :]) ** 2 + (control_points[2][:, None] - block_points[2][None, :]) ** 2
        basis_values = lax.rsqrt(1.0 + distance)
        return block_points[None] + jnp.einsum('mac,cn->man', chosen, basis_values, precision=HIGH)
    moved_blocks = lax.map(move_block, vertex_blocks)
    moved_points = moved_blocks.transpose(1, 2, 0, 3).reshape(VARIANTS, 3, VERTS)
    centroid, area, weight = panel_shape(moved_points, connectivity)
    hull_mask = (1 - free_flags).astype(jnp.float32)
    boundary = jnp.einsum('ka,man->mkn', load_velocity, area, precision=HIGH) * hull_mask[None, None, :]
    first_strengths = boundary.astype(jnp.bfloat16)
    kernel_scale = 1.0 / (4.0 * math.pi * math.sqrt(PANELS))
    induced = apply_influence(centroid, weight, first_strengths, kernel_scale)
    second_strengths = (first_strengths.astype(jnp.float32) + (boundary - induced)).astype(jnp.bfloat16)
    pressure = apply_influence(centroid, weight, second_strengths, kernel_scale)
    panel_force = pressure * (area[:, 2, :] * hull_mask[None, :])[:, None, :]
    station_index = station_owner[:, 0] * STATIONS + jnp.arange(PANELS, dtype=jnp.int32) % STATIONS
    station_loads = jax.ops.segment_sum(panel_force.reshape(-1, PANELS).T, station_index, num_segments=STATIONS_ALL)
    station_place = jnp.arange(STATIONS_ALL, dtype=jnp.float32)[:, None] / STATIONS_ALL
    running = jnp.cumsum(station_loads, axis=0)
    earlier = running - station_loads
    placed_loads = station_loads * station_place
    moment_arm = jnp.cumsum(placed_loads, axis=0) - placed_loads
    inv_root = 1.0 / math.sqrt(PANELS)
    shear = (running * inv_root).T.reshape(VARIANTS, LOADS, STATIONS_ALL)
    moment = ((station_place * earlier - moment_arm) * inv_root).T.reshape(VARIANTS, LOADS, STATIONS_ALL)
    return (shear, moment)
```

```python
import functools
import math

import jax
import jax.numpy as jnp
from jax import lax
from jax.experimental import pallas as pl
from jax.experimental.pallas import tpu as pltpu
from jax.sharding import PartitionSpec as P

STATIONS = 128


HIGH = lax.Precision.HIGHEST
CORE_SQUARE = 0.0025
SKIN_SQUARE = 0.01


def prefix(shard, axis, combine, identity):
    length, index = (lax.axis_size(axis), lax.axis_index(axis))
    everything = jax.tree.map(lambda part: lax.all_gather(part, axis), shard)
    start = jax.tree.map(
        lambda part, zero: jnp.broadcast_to(jnp.asarray(zero, part.dtype), part.shape),
        shard,
        identity,
    )

    def step(k, before):
        reached = k < index
        new = combine(before, jax.tree.map(lambda part: part[k], everything))
        return jax.tree.map(lambda a, b: jnp.where(reached, a, b), new, before)

    return lax.fori_loop(0, length, step, start)


def panel_shape(moved_points, corner_rows):
    first_corner = jnp.take(moved_points, corner_rows[0], axis=2)
    second_corner = jnp.take(moved_points, corner_rows[1], axis=2)
    third_corner = jnp.take(moved_points, corner_rows[2], axis=2)
    centroid = (first_corner + second_corner + third_corner) / 3.0
    edge_one = second_corner - first_corner
    edge_two = third_corner - first_corner
    cross_x = edge_one[:, 1] * edge_two[:, 2] - edge_one[:, 2] * edge_two[:, 1]
    cross_y = edge_one[:, 2] * edge_two[:, 0] - edge_one[:, 0] * edge_two[:, 2]
    cross_z = edge_one[:, 0] * edge_two[:, 1] - edge_one[:, 1] * edge_two[:, 0]
    area = 0.5 * jnp.stack([cross_x, cross_y, cross_z], axis=1)
    weight = jnp.sqrt(jnp.sum(area * area, axis=1) + SKIN_SQUARE)
    return (centroid, area, weight)


def tile_block(targets, sources, strengths, kernel_scale):
    distance = (
        (targets[:, 0, :, None] - sources[:, 0, None, :]) ** 2
        + (targets[:, 1, :, None] - sources[:, 1, None, :]) ** 2
        + (targets[:, 2, :, None] - sources[:, 2, None, :]) ** 2
    )
    influence = (sources[:, 3, None, :] * kernel_scale * lax.rsqrt(distance + CORE_SQUARE)).astype(
        jnp.bfloat16
    )
    return jnp.einsum("mrn,mkn->mkr", influence, strengths, preferred_element_type=jnp.float32)


def tile_product(carry_sum, targets, sources, strengths, kernel_scale):
    columns = strengths.shape[2]
    block_width = columns
    for candidate in (2048, 1024, 512):
        if columns > candidate and columns % candidate == 0:
            block_width = candidate
            break
    if block_width == columns:
        return carry_sum + tile_block(targets, sources, strengths, kernel_scale)

    def block_step(step_index, running_sum):
        column_start = step_index * block_width
        part_sources = lax.dynamic_slice_in_dim(sources, column_start, block_width, 2)
        part_strengths = lax.dynamic_slice_in_dim(strengths, column_start, block_width, 2)
        return running_sum + tile_block(targets, part_sources, part_strengths, kernel_scale)

    return lax.fori_loop(0, columns // block_width, block_step, carry_sum)


def add_pairs(earlier, later):
    return (earlier[0] + later[0], earlier[1] + later[1])


def shards(
    base_points,
    control_points,
    morph_weights,
    connectivity,
    free_flags,
    station_owner,
    variant_order,
    load_velocity,
):
    owners = lax.axis_size(("panels", "cols"))
    owner_index = lax.axis_index(("panels", "cols"))
    phase_index = lax.axis_index("phase")
    variant_dev = variant_order.shape[0] // lax.axis_size("phase")
    vert_dev = base_points.shape[1]
    pan_dev = connectivity.shape[1]
    load_count = load_velocity.shape[0]
    panels_total = pan_dev * owners
    own_variants = lax.dynamic_slice_in_dim(
        variant_order, phase_index * variant_dev, variant_dev, 0
    )
    picker = (
        own_variants[:, None] == jnp.arange(variant_order.shape[0], dtype=jnp.int32)[None, :]
    ).astype(jnp.float32)
    chosen = jnp.einsum("mv,vac->mac", picker, morph_weights, precision=HIGH)
    distance = (
        (control_points[0][:, None] - base_points[0][None, :]) ** 2
        + (control_points[1][:, None] - base_points[1][None, :]) ** 2
        + (control_points[2][:, None] - base_points[2][None, :]) ** 2
    )
    basis_values = lax.rsqrt(1.0 + distance)
    moved_points = base_points[None] + jnp.einsum(
        "mac,cn->man", chosen, basis_values, precision=HIGH
    )
    local_corners = connectivity - owner_index * vert_dev
    centroid, area, weight = panel_shape(moved_points, local_corners)
    hull_mask = (1 - free_flags).astype(jnp.float32)
    boundary = (
        jnp.einsum("ka,man->mkn", load_velocity, area, precision=HIGH) * hull_mask[None, None, :]
    )
    first_strengths = boundary.astype(jnp.bfloat16)
    kernel_scale = 1.0 / (4.0 * math.pi * math.sqrt(panels_total))
    own_geometry = jnp.concatenate([centroid, weight[:, None, :]], axis=1)
    sources = lax.all_gather(own_geometry, "panels", axis=2, tiled=True)
    row_targets = lax.all_gather(centroid, "cols", axis=2, tiled=True)

    def apply_influence(strengths):
        empty_sum = jnp.zeros((variant_dev, load_count, row_targets.shape[2]), jnp.float32)
        partial_sums = tile_product(
            empty_sum,
            row_targets,
            sources,
            lax.all_gather(strengths, "panels", axis=2, tiled=True),
            kernel_scale,
        )
        return lax.psum_scatter(partial_sums, "cols", scatter_dimension=2, tiled=True)

    induced = apply_influence(first_strengths)
    second_strengths = (first_strengths.astype(jnp.float32) + (boundary - induced)).astype(
        jnp.bfloat16
    )
    pressure = apply_influence(second_strengths)
    panel_force = pressure * (area[:, 2, :] * hull_mask[None, :])[:, None, :]
    force_rows = panel_force.reshape(-1, pan_dev)
    capacity = max(2, 5 * pan_dev // (2 * owners))
    target_owner = station_owner[:, 0]
    panel_order = jnp.arange(pan_dev, dtype=jnp.int32)
    ahead = (target_owner[:, None] == target_owner[None, :]) & (
        panel_order[None, :] < panel_order[:, None]
    )
    slot_rank = jnp.sum(ahead.astype(jnp.int32), axis=1)
    slot_index = target_owner * capacity + slot_rank
    all_slots = jnp.arange(owners * capacity, dtype=jnp.int32)
    placed = slot_index[:, None] == all_slots[None, :]
    send_values = jnp.dot(force_rows, placed.astype(jnp.float32), precision=HIGH)
    station_bins = (owner_index * pan_dev + panel_order) % STATIONS
    send_bins = jnp.max(jnp.where(placed, station_bins[:, None], -1), axis=0)[None, :]
    recv_values, recv_bins = (
        lax.all_to_all(send_values, ("panels", "cols"), split_axis=1, concat_axis=1, tiled=True),
        lax.all_to_all(send_bins, ("panels", "cols"), split_axis=1, concat_axis=1, tiled=True),
    )
    matches = (recv_bins[0][:, None] == jnp.arange(STATIONS, dtype=jnp.int32)[None, :]).astype(
        jnp.float32
    )
    station_loads = jnp.dot(recv_values, matches, precision=HIGH)
    station_place = (owner_index * STATIONS + jnp.arange(STATIONS, dtype=jnp.int32)).astype(
        jnp.float32
    ) / (STATIONS * owners)
    placed_loads = station_loads * station_place[None, :]
    own_total = jnp.sum(station_loads, axis=1)
    own_arm = jnp.sum(placed_loads, axis=1)
    zero_row = jnp.zeros_like(own_total)
    prior_total, prior_arm = prefix(
        (own_total, own_arm), ("panels", "cols"), add_pairs, (zero_row, zero_row)
    )
    station_rank = jnp.arange(STATIONS, dtype=jnp.int32)
    inclusive = (station_rank[:, None] <= station_rank[None, :]).astype(jnp.float32)
    strict = (station_rank[:, None] < station_rank[None, :]).astype(jnp.float32)
    running = prior_total[:, None] + jnp.dot(station_loads, inclusive, precision=HIGH)
    earlier = prior_total[:, None] + jnp.dot(station_loads, strict, precision=HIGH)
    moment_arm = prior_arm[:, None] + jnp.dot(placed_loads, strict, precision=HIGH)
    inv_root = 1.0 / math.sqrt(panels_total)
    shear = (running * inv_root).reshape(variant_dev, load_count, STATIONS)
    moment = ((station_place[None, :] * earlier - moment_arm) * inv_root).reshape(
        variant_dev, load_count, STATIONS
    )
    return (shear, moment)


TILE_ROWS = 8
LANES = 128
FUSED_PANELS = 1024


def own_geometry_rows(weights, points_col, corner_rows, control_ref, vert_dev):
    controls = control_ref.shape[1]
    chunk = min(controls, 2 * LANES)
    totals = [jnp.zeros((vert_dev, chunk), jnp.float32) for _ in range(3)]
    columns = [jnp.broadcast_to(col, (vert_dev, chunk)) for col in points_col]
    for start in range(0, controls, chunk):
        span = slice(start, start + chunk)
        dx = control_ref[0:1, span] - columns[0]
        dy = control_ref[1:2, span] - columns[1]
        dz = control_ref[2:3, span] - columns[2]
        basis = lax.rsqrt(1.0 + (dx * dx + dy * dy + dz * dz))
        totals = [totals[a] + weights[a : a + 1, span] * basis for a in range(3)]
    moved = [points_col[a] + jnp.sum(totals[a], axis=1, keepdims=True) for a in range(3)]
    vertex = lax.broadcasted_iota(jnp.int32, (vert_dev, corner_rows.shape[1]), 0)
    corners = []
    for q in range(3):
        hit = vertex == corner_rows[q : q + 1, :]
        corners.append(
            [jnp.sum(jnp.where(hit, moved[a], 0.0), axis=0, keepdims=True) for a in range(3)]
        )
    p0, p1, p2 = corners
    centroid = [(p0[a] + p1[a] + p2[a]) / 3.0 for a in range(3)]
    e1 = [p1[a] - p0[a] for a in range(3)]
    e2 = [p2[a] - p0[a] for a in range(3)]
    area = [
        0.5 * (e1[1] * e2[2] - e1[2] * e2[1]),
        0.5 * (e1[2] * e2[0] - e1[0] * e2[2]),
        0.5 * (e1[0] * e2[1] - e1[1] * e2[0]),
    ]
    weight = jnp.sqrt(area[0] * area[0] + area[1] * area[1] + area[2] * area[2] + SKIN_SQUARE)
    return centroid, weight, area


def fused_kernel(
    panels_axis,
    cols_axis,
    order_ref,
    base_hbm,
    control_hbm,
    morph_hbm,
    corner_hbm,
    flag_hbm,
    owner_hbm,
    velocity_hbm,
    shear_ref,
    moment_ref,
    base_ref,
    control_ref,
    morph_ref,
    corner_ref,
    flag_ref,
    owner_ref,
    velocity_ref,
    mix_ref,
    gathered,
    influence_ref,
    in_sem,
    send_sem,
    recv_sem,
):
    owners = panels_axis * cols_axis
    row, col = lax.axis_index("panels"), lax.axis_index("cols")
    me = row * cols_axis + col
    vert_dev = base_ref.shape[1]
    pan_dev = corner_ref.shape[1]
    loads = velocity_ref.shape[1]
    panels_total = pan_dev * owners

    def peer_of(offset):
        peer = lax.rem(me + offset, owners)
        return {"panels": peer // cols_axis, "cols": lax.rem(peer, cols_axis)}

    barrier = pltpu.get_barrier_semaphore()
    for offset in range(1, owners):
        pl.semaphore_signal(
            barrier, inc=1, device_id=peer_of(offset), device_id_type=pl.DeviceIdType.MESH
        )
    pairs = (
        (base_hbm, base_ref),
        (control_hbm, control_ref),
        (morph_hbm, morph_ref),
        (corner_hbm, corner_ref),
        (flag_hbm, flag_ref),
        (owner_hbm, owner_ref),
        (velocity_hbm, velocity_ref),
    )
    fetches = [
        pltpu.make_async_copy(source, target, in_sem.at[k])
        for k, (source, target) in enumerate(pairs)
    ]
    for fetch in fetches:
        fetch.start()
    mix_ref[...] = jnp.zeros(mix_ref.shape, jnp.float32)
    for fetch in fetches:
        fetch.wait()

    mix_ref[0:3, 0:loads] = velocity_ref[...]
    mix_ref[0:3, LANES : LANES + vert_dev] = base_ref[...]
    mixed = mix_ref[...].T
    velocity_col = [mixed[0:loads, a : a + 1] for a in range(3)]
    points_col = [mixed[LANES : LANES + vert_dev, a : a + 1] for a in range(3)]
    weights = morph_ref[order_ref[lax.axis_index("phase")]]
    centroid, weight, area = own_geometry_rows(
        weights, points_col, corner_ref[...] - me * vert_dev, control_ref, vert_dev
    )
    hull = (1 - flag_ref[...]).astype(jnp.float32)
    station = (
        owner_ref[...] * STATIONS
        + lax.rem(me * pan_dev, STATIONS)
        + lax.broadcasted_iota(jnp.int32, (1, pan_dev), 1)
    ).astype(jnp.float32)
    rows = centroid + [weight] + [part * hull for part in area] + [station]
    gathered[me, :, 0:pan_dev] = jnp.concatenate(rows, axis=0)

    pl.semaphore_wait(barrier, owners - 1)
    sends = []
    for offset in range(1, owners):
        send = pltpu.make_async_remote_copy(
            src_ref=gathered.at[me],
            dst_ref=gathered.at[me],
            send_sem=send_sem.at[offset - 1],
            recv_sem=recv_sem.at[me],
            device_id=peer_of(offset),
            device_id_type=pl.DeviceIdType.MESH,
        )
        send.start()
        sends.append(send)
    for offset in range(1, owners):
        source = lax.rem(me + offset, owners)
        pltpu.make_async_remote_copy(
            src_ref=gathered.at[source],
            dst_ref=gathered.at[source],
            send_sem=send_sem.at[offset - 1],
            recv_sem=recv_sem.at[source],
            device_id=peer_of(offset),
            device_id_type=pl.DeviceIdType.MESH,
        ).wait_recv()

    rows = jnp.concatenate([gathered[d, :, 0:pan_dev] for d in range(owners)], axis=1)
    columns = rows.T
    kernel_scale = 1.0 / (4.0 * math.pi * math.sqrt(panels_total))
    block = 32
    for start in range(0, panels_total, block):
        part = columns[start : start + block]
        dx = rows[0:1] - part[:, 0:1]
        dy = rows[1:2] - part[:, 1:2]
        dz = rows[2:3] - part[:, 2:3]
        distance = dx * dx + dy * dy + dz * dz
        influence_ref[start : start + block, :] = (
            (part[:, 3:4] * kernel_scale) * lax.rsqrt(distance + CORE_SQUARE)
        ).astype(jnp.bfloat16)
    boundary = (
        velocity_col[0] * rows[4:5] + velocity_col[1] * rows[5:6] + velocity_col[2] * rows[6:7]
    )
    first = boundary.astype(jnp.bfloat16)
    induced = jnp.dot(first, influence_ref[...], preferred_element_type=jnp.float32)
    second = (first.astype(jnp.float32) + (boundary - induced)).astype(jnp.bfloat16)
    pressure = jnp.dot(second, influence_ref[...], preferred_element_type=jnp.float32)
    force = pressure * rows[6:7]
    force_high = force.astype(jnp.bfloat16)
    force_low = (force - force_high.astype(jnp.float32)).astype(jnp.bfloat16)
    here = (
        me * STATIONS + lax.broadcasted_iota(jnp.int32, (panels_total, STATIONS), 1)
    ).astype(jnp.float32)
    gap = here - columns[:, 7:8]
    reached = jnp.where(gap >= 0.0, 1.0, 0.0).astype(jnp.bfloat16)
    arm = jnp.maximum(gap, 0.0)
    arm_high = arm.astype(jnp.bfloat16)
    arm_low = (arm - arm_high.astype(jnp.float32)).astype(jnp.bfloat16)
    summed = jnp.dot(
        jnp.concatenate([force_high, force_low], axis=0),
        jnp.concatenate([reached, arm_high, arm_low], axis=1),
        preferred_element_type=jnp.float32,
    )
    summed = summed[0:loads] + summed[loads : 2 * loads]
    inv_root = 1.0 / math.sqrt(panels_total)
    shear_ref[0] = summed[:, 0:STATIONS] * inv_root
    moment_ref[0] = (summed[:, STATIONS : 2 * STATIONS] + summed[:, 2 * STATIONS :]) * (
        inv_root / (STATIONS * owners)
    )
    for send in sends:
        send.wait_send()


def fused_shards(
    panels_axis,
    cols_axis,
    base_points,
    control_points,
    morph_weights,
    connectivity,
    free_flags,
    station_owner,
    variant_order,
    load_velocity,
):
    owners = panels_axis * cols_axis
    pan_dev = connectivity.shape[1]
    loads = load_velocity.shape[0]
    panels_total = pan_dev * owners
    hbm_inputs = (
        base_points,
        control_points,
        morph_weights,
        connectivity,
        free_flags.reshape(1, pan_dev),
        station_owner.reshape(1, pan_dev),
        load_velocity.T,
    )
    result = jax.ShapeDtypeStruct((1, loads, STATIONS), jnp.float32)
    return tuple(
        pl.pallas_call(
            functools.partial(fused_kernel, panels_axis, cols_axis),
            out_shape=(result, result),
            in_specs=[pl.BlockSpec(memory_space=pltpu.SMEM)]
            + [pl.BlockSpec(memory_space=pltpu.HBM)] * len(hbm_inputs),
            out_specs=(pl.BlockSpec(memory_space=pltpu.VMEM),) * 2,
            scratch_shapes=[pltpu.VMEM(part.shape, part.dtype) for part in hbm_inputs]
            + [
                pltpu.VMEM((TILE_ROWS, 2 * LANES), jnp.float32),
                pltpu.VMEM((owners, TILE_ROWS, LANES), jnp.float32),
                pltpu.VMEM((panels_total, panels_total), jnp.bfloat16),
                pltpu.SemaphoreType.DMA((len(hbm_inputs),)),
                pltpu.SemaphoreType.DMA((owners,)),
                pltpu.SemaphoreType.DMA((owners,)),
            ],
            compiler_params=pltpu.CompilerParams(collective_id=0, has_side_effects=True),
        )(variant_order, *hbm_inputs)
    )


def choose_shards(mesh, *arrays):
    panels_axis, cols_axis = mesh.shape["panels"], mesh.shape["cols"]
    owners = panels_axis * cols_axis
    base_points, connectivity, variant_order, load_velocity = (
        arrays[0],
        arrays[3],
        arrays[6],
        arrays[7],
    )
    pan_dev = connectivity.shape[1]
    fits = (
        pan_dev * owners <= FUSED_PANELS
        and pan_dev <= LANES
        and STATIONS % pan_dev == 0
        and base_points.shape[1] <= LANES
        and load_velocity.shape[0] <= LANES
        and variant_order.shape[0] == mesh.shape["phase"]
    )
    if fits:
        return fused_shards(panels_axis, cols_axis, *arrays)
    return shards(*arrays)


def solution(mesh):
    return jax.shard_map(
        functools.partial(choose_shards, mesh),
        mesh=mesh,
        in_specs=(
            P(None, ("groups", "panels", "cols")),
            P(),
            P("groups", None, None),
            P(None, ("groups", "panels", "cols")),
            P(("groups", "panels", "cols")),
            P(("groups", "panels", "cols"), None),
            P("groups"),
            P(),
        ),
        out_specs=(
            P(("groups", "phase"), None, ("panels", "cols")),
            P(("groups", "phase"), None, ("panels", "cols")),
        ),
        check_vma=False,
    )
```

```python
import functools
import math

import jax
import jax.numpy as jnp
from jax import lax
from jax.experimental import pallas as pl
from jax.experimental.pallas import tpu as pltpu
from jax.sharding import PartitionSpec as P

STATIONS = 128


HIGH = lax.Precision.HIGHEST
CORE_SQUARE = 0.0025
SKIN_SQUARE = 0.01


def prefix(shard, axis, combine, identity):
    length, index = (lax.axis_size(axis), lax.axis_index(axis))
    everything = jax.tree.map(lambda part: lax.all_gather(part, axis), shard)
    start = jax.tree.map(
        lambda part, zero: jnp.broadcast_to(jnp.asarray(zero, part.dtype), part.shape),
        shard,
        identity,
    )

    def step(k, before):
        reached = k < index
        new = combine(before, jax.tree.map(lambda part: part[k], everything))
        return jax.tree.map(lambda a, b: jnp.where(reached, a, b), new, before)

    return lax.fori_loop(0, length, step, start)


def panel_shape(moved_points, corner_rows):
    first_corner = jnp.take(moved_points, corner_rows[0], axis=2)
    second_corner = jnp.take(moved_points, corner_rows[1], axis=2)
    third_corner = jnp.take(moved_points, corner_rows[2], axis=2)
    centroid = (first_corner + second_corner + third_corner) / 3.0
    edge_one = second_corner - first_corner
    edge_two = third_corner - first_corner
    cross_x = edge_one[:, 1] * edge_two[:, 2] - edge_one[:, 2] * edge_two[:, 1]
    cross_y = edge_one[:, 2] * edge_two[:, 0] - edge_one[:, 0] * edge_two[:, 2]
    cross_z = edge_one[:, 0] * edge_two[:, 1] - edge_one[:, 1] * edge_two[:, 0]
    area = 0.5 * jnp.stack([cross_x, cross_y, cross_z], axis=1)
    weight = jnp.sqrt(jnp.sum(area * area, axis=1) + SKIN_SQUARE)
    return (centroid, area, weight)


def tile_block(targets, sources, strengths, kernel_scale):
    distance = (
        (targets[:, 0, :, None] - sources[:, 0, None, :]) ** 2
        + (targets[:, 1, :, None] - sources[:, 1, None, :]) ** 2
        + (targets[:, 2, :, None] - sources[:, 2, None, :]) ** 2
    )
    influence = (sources[:, 3, None, :] * kernel_scale * lax.rsqrt(distance + CORE_SQUARE)).astype(
        jnp.bfloat16
    )
    return jnp.einsum("mrn,mkn->mkr", influence, strengths, preferred_element_type=jnp.float32)


def tile_product(carry_sum, targets, sources, strengths, kernel_scale):
    columns = strengths.shape[2]
    block_width = columns
    for candidate in (2048, 1024, 512):
        if columns > candidate and columns % candidate == 0:
            block_width = candidate
            break
    if block_width == columns:
        return carry_sum + tile_block(targets, sources, strengths, kernel_scale)

    def block_step(step_index, running_sum):
        column_start = step_index * block_width
        part_sources = lax.dynamic_slice_in_dim(sources, column_start, block_width, 2)
        part_strengths = lax.dynamic_slice_in_dim(strengths, column_start, block_width, 2)
        return running_sum + tile_block(targets, part_sources, part_strengths, kernel_scale)

    return lax.fori_loop(0, columns // block_width, block_step, carry_sum)


def add_pairs(earlier, later):
    return (earlier[0] + later[0], earlier[1] + later[1])


def shards(
    base_points,
    control_points,
    morph_weights,
    connectivity,
    free_flags,
    station_owner,
    variant_order,
    load_velocity,
):
    owners = lax.axis_size(("panels", "cols"))
    owner_index = lax.axis_index(("panels", "cols"))
    phase_index = lax.axis_index("phase")
    variant_dev = variant_order.shape[0] // lax.axis_size("phase")
    vert_dev = base_points.shape[1]
    pan_dev = connectivity.shape[1]
    load_count = load_velocity.shape[0]
    panels_total = pan_dev * owners
    own_variants = lax.dynamic_slice_in_dim(
        variant_order, phase_index * variant_dev, variant_dev, 0
    )
    picker = (
        own_variants[:, None] == jnp.arange(variant_order.shape[0], dtype=jnp.int32)[None, :]
    ).astype(jnp.float32)
    chosen = jnp.einsum("mv,vac->mac", picker, morph_weights, precision=HIGH)
    distance = (
        (control_points[0][:, None] - base_points[0][None, :]) ** 2
        + (control_points[1][:, None] - base_points[1][None, :]) ** 2
        + (control_points[2][:, None] - base_points[2][None, :]) ** 2
    )
    basis_values = lax.rsqrt(1.0 + distance)
    moved_points = base_points[None] + jnp.einsum(
        "mac,cn->man", chosen, basis_values, precision=HIGH
    )
    local_corners = connectivity - owner_index * vert_dev
    centroid, area, weight = panel_shape(moved_points, local_corners)
    hull_mask = (1 - free_flags).astype(jnp.float32)
    boundary = (
        jnp.einsum("ka,man->mkn", load_velocity, area, precision=HIGH) * hull_mask[None, None, :]
    )
    first_strengths = boundary.astype(jnp.bfloat16)
    kernel_scale = 1.0 / (4.0 * math.pi * math.sqrt(panels_total))
    own_geometry = jnp.concatenate([centroid, weight[:, None, :]], axis=1)
    sources = lax.all_gather(own_geometry, "panels", axis=2, tiled=True)
    row_targets = lax.all_gather(centroid, "cols", axis=2, tiled=True)

    def apply_influence(strengths):
        empty_sum = jnp.zeros((variant_dev, load_count, row_targets.shape[2]), jnp.float32)
        partial_sums = tile_product(
            empty_sum,
            row_targets,
            sources,
            lax.all_gather(strengths, "panels", axis=2, tiled=True),
            kernel_scale,
        )
        return lax.psum_scatter(partial_sums, "cols", scatter_dimension=2, tiled=True)

    induced = apply_influence(first_strengths)
    second_strengths = (first_strengths.astype(jnp.float32) + (boundary - induced)).astype(
        jnp.bfloat16
    )
    pressure = apply_influence(second_strengths)
    panel_force = pressure * (area[:, 2, :] * hull_mask[None, :])[:, None, :]
    force_rows = panel_force.reshape(-1, pan_dev)
    capacity = max(2, 5 * pan_dev // (2 * owners))
    target_owner = station_owner[:, 0]
    panel_order = jnp.arange(pan_dev, dtype=jnp.int32)
    ahead = (target_owner[:, None] == target_owner[None, :]) & (
        panel_order[None, :] < panel_order[:, None]
    )
    slot_rank = jnp.sum(ahead.astype(jnp.int32), axis=1)
    slot_index = target_owner * capacity + slot_rank
    all_slots = jnp.arange(owners * capacity, dtype=jnp.int32)
    placed = slot_index[:, None] == all_slots[None, :]
    send_values = jnp.dot(force_rows, placed.astype(jnp.float32), precision=HIGH)
    station_bins = (owner_index * pan_dev + panel_order) % STATIONS
    send_bins = jnp.max(jnp.where(placed, station_bins[:, None], -1), axis=0)[None, :]
    recv_values, recv_bins = (
        lax.all_to_all(send_values, ("panels", "cols"), split_axis=1, concat_axis=1, tiled=True),
        lax.all_to_all(send_bins, ("panels", "cols"), split_axis=1, concat_axis=1, tiled=True),
    )
    matches = (recv_bins[0][:, None] == jnp.arange(STATIONS, dtype=jnp.int32)[None, :]).astype(
        jnp.float32
    )
    station_loads = jnp.dot(recv_values, matches, precision=HIGH)
    station_place = (owner_index * STATIONS + jnp.arange(STATIONS, dtype=jnp.int32)).astype(
        jnp.float32
    ) / (STATIONS * owners)
    placed_loads = station_loads * station_place[None, :]
    own_total = jnp.sum(station_loads, axis=1)
    own_arm = jnp.sum(placed_loads, axis=1)
    zero_row = jnp.zeros_like(own_total)
    prior_total, prior_arm = prefix(
        (own_total, own_arm), ("panels", "cols"), add_pairs, (zero_row, zero_row)
    )
    station_rank = jnp.arange(STATIONS, dtype=jnp.int32)
    inclusive = (station_rank[:, None] <= station_rank[None, :]).astype(jnp.float32)
    strict = (station_rank[:, None] < station_rank[None, :]).astype(jnp.float32)
    running = prior_total[:, None] + jnp.dot(station_loads, inclusive, precision=HIGH)
    earlier = prior_total[:, None] + jnp.dot(station_loads, strict, precision=HIGH)
    moment_arm = prior_arm[:, None] + jnp.dot(placed_loads, strict, precision=HIGH)
    inv_root = 1.0 / math.sqrt(panels_total)
    shear = (running * inv_root).reshape(variant_dev, load_count, STATIONS)
    moment = ((station_place[None, :] * earlier - moment_arm) * inv_root).reshape(
        variant_dev, load_count, STATIONS
    )
    return (shear, moment)


TILE_ROWS = 8
LANES = 128
LOAD_GRANT = 16 << 20
FUSED_PANELS = 1024


def own_geometry_rows(weights, points_col, corner_rows, control_ref, vert_dev):
    controls = control_ref.shape[1]
    chunk = min(controls, 2 * LANES)
    totals = [jnp.zeros((vert_dev, chunk), jnp.float32) for _ in range(3)]
    columns = [jnp.broadcast_to(col, (vert_dev, chunk)) for col in points_col]
    for start in range(0, controls, chunk):
        span = slice(start, start + chunk)
        dx = control_ref[0:1, span] - columns[0]
        dy = control_ref[1:2, span] - columns[1]
        dz = control_ref[2:3, span] - columns[2]
        basis = lax.rsqrt(1.0 + (dx * dx + dy * dy + dz * dz))
        totals = [totals[a] + weights[a : a + 1, span] * basis for a in range(3)]
    moved = [points_col[a] + jnp.sum(totals[a], axis=1, keepdims=True) for a in range(3)]
    vertex = lax.broadcasted_iota(jnp.int32, (vert_dev, corner_rows.shape[1]), 0)
    corners = []
    for q in range(3):
        hit = vertex == corner_rows[q : q + 1, :]
        corners.append(
            [jnp.sum(jnp.where(hit, moved[a], 0.0), axis=0, keepdims=True) for a in range(3)]
        )
    p0, p1, p2 = corners
    centroid = [(p0[a] + p1[a] + p2[a]) / 3.0 for a in range(3)]
    e1 = [p1[a] - p0[a] for a in range(3)]
    e2 = [p2[a] - p0[a] for a in range(3)]
    area = [
        0.5 * (e1[1] * e2[2] - e1[2] * e2[1]),
        0.5 * (e1[2] * e2[0] - e1[0] * e2[2]),
        0.5 * (e1[0] * e2[1] - e1[1] * e2[0]),
    ]
    weight = jnp.sqrt(area[0] * area[0] + area[1] * area[1] + area[2] * area[2] + SKIN_SQUARE)
    return centroid, weight, area


def gather_kernel(
    panels_axis,
    cols_axis,
    order_ref,
    base_hbm,
    control_hbm,
    morph_hbm,
    corner_hbm,
    flag_hbm,
    owner_hbm,
    velocity_hbm,
    gathered,
    base_ref,
    control_ref,
    morph_ref,
    corner_ref,
    flag_ref,
    owner_ref,
    velocity_ref,
    mix_ref,
    in_sem,
    send_sem,
    recv_sem,
):
    owners = panels_axis * cols_axis
    row, col = lax.axis_index("panels"), lax.axis_index("cols")
    me = row * cols_axis + col
    vert_dev = base_ref.shape[1]
    pan_dev = corner_ref.shape[1]
    loads = velocity_ref.shape[1]

    def peer_of(offset):
        peer = lax.rem(me + offset, owners)
        return {"panels": peer // cols_axis, "cols": lax.rem(peer, cols_axis)}

    barrier = pltpu.get_barrier_semaphore()
    for offset in range(1, owners):
        pl.semaphore_signal(
            barrier, inc=1, device_id=peer_of(offset), device_id_type=pl.DeviceIdType.MESH
        )
    pairs = (
        (base_hbm, base_ref),
        (control_hbm, control_ref),
        (morph_hbm, morph_ref),
        (corner_hbm, corner_ref),
        (flag_hbm, flag_ref),
        (owner_hbm, owner_ref),
        (velocity_hbm, velocity_ref),
    )
    fetches = [
        pltpu.make_async_copy(source, target, in_sem.at[k])
        for k, (source, target) in enumerate(pairs)
    ]
    for fetch in fetches:
        fetch.start()
    mix_ref[...] = jnp.zeros(mix_ref.shape, jnp.float32)
    for fetch in fetches:
        fetch.wait()

    mix_ref[0:3, 0:vert_dev] = base_ref[...]
    mixed = mix_ref[...].T
    points_col = [mixed[0:vert_dev, a : a + 1] for a in range(3)]
    gathered[owners] = jnp.zeros((TILE_ROWS, LANES), jnp.float32)
    gathered[owners, 0:3, 0:loads] = velocity_ref[...]
    slot = order_ref[lax.axis_index("phase")]
    weights = jnp.concatenate([morph_ref[a, pl.ds(slot, 1), :] for a in range(3)], axis=0)
    centroid, weight, area = own_geometry_rows(
        weights, points_col, corner_ref[...] - me * vert_dev, control_ref, vert_dev
    )
    hull = (1 - flag_ref[...]).astype(jnp.float32)
    station = (
        owner_ref[...] * STATIONS
        + lax.rem(me * pan_dev, STATIONS)
        + lax.broadcasted_iota(jnp.int32, (1, pan_dev), 1)
    ).astype(jnp.float32)
    rows = centroid + [weight] + [part * hull for part in area] + [station]
    gathered[me, :, 0:pan_dev] = jnp.concatenate(rows, axis=0)

    pl.semaphore_wait(barrier, owners - 1)
    sends = []
    for offset in range(1, owners):
        send = pltpu.make_async_remote_copy(
            src_ref=gathered.at[me],
            dst_ref=gathered.at[me],
            send_sem=send_sem.at[offset - 1],
            recv_sem=recv_sem.at[me],
            device_id=peer_of(offset),
            device_id_type=pl.DeviceIdType.MESH,
        )
        send.start()
        sends.append(send)
    for offset in range(1, owners):
        source = lax.rem(me + offset, owners)
        pltpu.make_async_remote_copy(
            src_ref=gathered.at[source],
            dst_ref=gathered.at[source],
            send_sem=send_sem.at[offset - 1],
            recv_sem=recv_sem.at[source],
            device_id=peer_of(offset),
            device_id_type=pl.DeviceIdType.MESH,
        ).wait_recv()

    for send in sends:
        send.wait_send()


def load_kernel(panels_axis, cols_axis, pan_dev, loads, gathered, shear_ref, moment_ref, influence_ref):
    owners = panels_axis * cols_axis
    me = lax.axis_index("panels") * cols_axis + lax.axis_index("cols")
    panels_total = pan_dev * owners
    spread = gathered[owners].T
    velocity_col = [spread[0:loads, a : a + 1] for a in range(3)]
    rows = jnp.concatenate([gathered[d, :, 0:pan_dev] for d in range(owners)], axis=1)
    columns = rows.T
    kernel_scale = 1.0 / (4.0 * math.pi * math.sqrt(panels_total))
    block = 32
    for start in range(0, panels_total, block):
        part = columns[start : start + block]
        dx = rows[0:1] - part[:, 0:1]
        dy = rows[1:2] - part[:, 1:2]
        dz = rows[2:3] - part[:, 2:3]
        distance = dx * dx + dy * dy + dz * dz
        influence_ref[start : start + block, :] = (
            (part[:, 3:4] * kernel_scale) * lax.rsqrt(distance + CORE_SQUARE)
        ).astype(jnp.bfloat16)
    boundary = (
        velocity_col[0] * rows[4:5] + velocity_col[1] * rows[5:6] + velocity_col[2] * rows[6:7]
    )
    first = boundary.astype(jnp.bfloat16)
    induced = jnp.dot(first, influence_ref[...], preferred_element_type=jnp.float32)
    second = (first.astype(jnp.float32) + (boundary - induced)).astype(jnp.bfloat16)
    pressure = jnp.dot(second, influence_ref[...], preferred_element_type=jnp.float32)
    force = pressure * rows[6:7]
    force_high = force.astype(jnp.bfloat16)
    force_low = (force - force_high.astype(jnp.float32)).astype(jnp.bfloat16)
    here = (
        me * STATIONS + lax.broadcasted_iota(jnp.int32, (panels_total, STATIONS), 1)
    ).astype(jnp.float32)
    gap = here - columns[:, 7:8]
    reached = jnp.where(gap >= 0.0, 1.0, 0.0).astype(jnp.bfloat16)
    arm = jnp.maximum(gap, 0.0)
    arm_high = arm.astype(jnp.bfloat16)
    arm_low = (arm - arm_high.astype(jnp.float32)).astype(jnp.bfloat16)
    summed = jnp.dot(
        jnp.concatenate([force_high, force_low], axis=0),
        jnp.concatenate([reached, arm_high, arm_low], axis=1),
        preferred_element_type=jnp.float32,
    )
    summed = summed[0:loads] + summed[loads : 2 * loads]
    inv_root = 1.0 / math.sqrt(panels_total)
    shear_ref[0] = summed[:, 0:STATIONS] * inv_root
    moment_ref[0] = (summed[:, STATIONS : 2 * STATIONS] + summed[:, 2 * STATIONS :]) * (
        inv_root / (STATIONS * owners)
    )


def fused_shards(
    panels_axis,
    cols_axis,
    base_points,
    control_points,
    morph_weights,
    connectivity,
    free_flags,
    station_owner,
    variant_order,
    load_velocity,
):
    owners = panels_axis * cols_axis
    pan_dev = connectivity.shape[1]
    loads = load_velocity.shape[0]
    panels_total = pan_dev * owners
    hbm_inputs = (
        base_points,
        control_points,
        morph_weights.transpose(1, 0, 2),
        connectivity,
        free_flags.reshape(1, pan_dev),
        station_owner.reshape(1, pan_dev),
        load_velocity.T,
    )
    gathered = pl.pallas_call(
        functools.partial(gather_kernel, panels_axis, cols_axis),
        out_shape=pltpu.VMEM((owners + 1, TILE_ROWS, LANES), jnp.float32),
        in_specs=[pl.BlockSpec(memory_space=pltpu.SMEM)]
        + [pl.BlockSpec(memory_space=pltpu.HBM)] * len(hbm_inputs),
        out_specs=pl.BlockSpec(memory_space=pltpu.VMEM),
        scratch_shapes=[pltpu.VMEM(part.shape, part.dtype) for part in hbm_inputs]
        + [
            pltpu.VMEM((TILE_ROWS, LANES), jnp.float32),
            pltpu.SemaphoreType.DMA((len(hbm_inputs),)),
            pltpu.SemaphoreType.DMA((owners,)),
            pltpu.SemaphoreType.DMA((owners,)),
        ],
        compiler_params=pltpu.CompilerParams(
            collective_id=0, has_side_effects=True
        ),
    )(variant_order, *hbm_inputs)
    result = jax.ShapeDtypeStruct((1, loads, STATIONS), jnp.float32)
    return tuple(
        pl.pallas_call(
            functools.partial(load_kernel, panels_axis, cols_axis, pan_dev, loads),
            out_shape=(result, result),
            in_specs=[pl.BlockSpec(memory_space=pltpu.VMEM)],
            out_specs=(pl.BlockSpec(memory_space=pltpu.VMEM),) * 2,
            scratch_shapes=[pltpu.VMEM((panels_total, panels_total), jnp.bfloat16)],
            compiler_params=pltpu.CompilerParams(vmem_limit_bytes=LOAD_GRANT),
        )(gathered)
    )


def choose_shards(mesh, *arrays):
    panels_axis, cols_axis = mesh.shape["panels"], mesh.shape["cols"]
    owners = panels_axis * cols_axis
    base_points, connectivity, variant_order, load_velocity = (
        arrays[0],
        arrays[3],
        arrays[6],
        arrays[7],
    )
    pan_dev = connectivity.shape[1]
    fits = (
        pan_dev * owners <= FUSED_PANELS
        and pan_dev <= LANES
        and STATIONS % pan_dev == 0
        and base_points.shape[1] <= LANES
        and load_velocity.shape[0] <= LANES
        and variant_order.shape[0] == mesh.shape["phase"]
    )
    if fits:
        return fused_shards(panels_axis, cols_axis, *arrays)
    return shards(*arrays)


def solution(mesh):
    return jax.shard_map(
        functools.partial(choose_shards, mesh),
        mesh=mesh,
        in_specs=(
            P(None, ("groups", "panels", "cols")),
            P(),
            P("groups", None, None),
            P(None, ("groups", "panels", "cols")),
            P(("groups", "panels", "cols")),
            P(("groups", "panels", "cols"), None),
            P("groups"),
            P(),
        ),
        out_specs=(
            P(("groups", "phase"), None, ("panels", "cols")),
            P(("groups", "phase"), None, ("panels", "cols")),
        ),
        check_vma=False,
    )
```

```python
import functools
import math

import jax
import jax.numpy as jnp
from jax import lax
from jax.experimental import pallas as pl
from jax.experimental.pallas import tpu as pltpu
from jax.sharding import PartitionSpec as P

STATIONS = 128


HIGH = lax.Precision.HIGHEST
CORE_SQUARE = 0.0025
SKIN_SQUARE = 0.01


def prefix(shard, axis, combine, identity):
    length, index = (lax.axis_size(axis), lax.axis_index(axis))
    everything = jax.tree.map(lambda part: lax.all_gather(part, axis), shard)
    start = jax.tree.map(
        lambda part, zero: jnp.broadcast_to(jnp.asarray(zero, part.dtype), part.shape),
        shard,
        identity,
    )

    def step(k, before):
        reached = k < index
        new = combine(before, jax.tree.map(lambda part: part[k], everything))
        return jax.tree.map(lambda a, b: jnp.where(reached, a, b), new, before)

    return lax.fori_loop(0, length, step, start)


def panel_shape(moved_points, corner_rows):
    first_corner = jnp.take(moved_points, corner_rows[0], axis=2)
    second_corner = jnp.take(moved_points, corner_rows[1], axis=2)
    third_corner = jnp.take(moved_points, corner_rows[2], axis=2)
    centroid = (first_corner + second_corner + third_corner) / 3.0
    edge_one = second_corner - first_corner
    edge_two = third_corner - first_corner
    cross_x = edge_one[:, 1] * edge_two[:, 2] - edge_one[:, 2] * edge_two[:, 1]
    cross_y = edge_one[:, 2] * edge_two[:, 0] - edge_one[:, 0] * edge_two[:, 2]
    cross_z = edge_one[:, 0] * edge_two[:, 1] - edge_one[:, 1] * edge_two[:, 0]
    area = 0.5 * jnp.stack([cross_x, cross_y, cross_z], axis=1)
    weight = jnp.sqrt(jnp.sum(area * area, axis=1) + SKIN_SQUARE)
    return (centroid, area, weight)


def tile_block(targets, sources, strengths, kernel_scale):
    distance = (
        (targets[:, 0, :, None] - sources[:, 0, None, :]) ** 2
        + (targets[:, 1, :, None] - sources[:, 1, None, :]) ** 2
        + (targets[:, 2, :, None] - sources[:, 2, None, :]) ** 2
    )
    influence = (sources[:, 3, None, :] * kernel_scale * lax.rsqrt(distance + CORE_SQUARE)).astype(
        jnp.bfloat16
    )
    return jnp.einsum("mrn,mkn->mkr", influence, strengths, preferred_element_type=jnp.float32)


def tile_product(carry_sum, targets, sources, strengths, kernel_scale):
    columns = strengths.shape[2]
    block_width = columns
    for candidate in (2048, 1024, 512):
        if columns > candidate and columns % candidate == 0:
            block_width = candidate
            break
    if block_width == columns:
        return carry_sum + tile_block(targets, sources, strengths, kernel_scale)

    def block_step(step_index, running_sum):
        column_start = step_index * block_width
        part_sources = lax.dynamic_slice_in_dim(sources, column_start, block_width, 2)
        part_strengths = lax.dynamic_slice_in_dim(strengths, column_start, block_width, 2)
        return running_sum + tile_block(targets, part_sources, part_strengths, kernel_scale)

    return lax.fori_loop(0, columns // block_width, block_step, carry_sum)


def add_pairs(earlier, later):
    return (earlier[0] + later[0], earlier[1] + later[1])


def shards(
    base_points,
    control_points,
    morph_weights,
    connectivity,
    free_flags,
    station_owner,
    variant_order,
    load_velocity,
):
    owners = lax.axis_size(("panels", "cols"))
    owner_index = lax.axis_index(("panels", "cols"))
    phase_index = lax.axis_index("phase")
    variant_dev = variant_order.shape[0] // lax.axis_size("phase")
    vert_dev = base_points.shape[1]
    pan_dev = connectivity.shape[1]
    load_count = load_velocity.shape[0]
    panels_total = pan_dev * owners
    own_variants = lax.dynamic_slice_in_dim(
        variant_order, phase_index * variant_dev, variant_dev, 0
    )
    picker = (
        own_variants[:, None] == jnp.arange(variant_order.shape[0], dtype=jnp.int32)[None, :]
    ).astype(jnp.float32)
    chosen = jnp.einsum("mv,vac->mac", picker, morph_weights, precision=HIGH)
    distance = (
        (control_points[0][:, None] - base_points[0][None, :]) ** 2
        + (control_points[1][:, None] - base_points[1][None, :]) ** 2
        + (control_points[2][:, None] - base_points[2][None, :]) ** 2
    )
    basis_values = lax.rsqrt(1.0 + distance)
    moved_points = base_points[None] + jnp.einsum(
        "mac,cn->man", chosen, basis_values, precision=HIGH
    )
    local_corners = connectivity - owner_index * vert_dev
    centroid, area, weight = panel_shape(moved_points, local_corners)
    hull_mask = (1 - free_flags).astype(jnp.float32)
    boundary = (
        jnp.einsum("ka,man->mkn", load_velocity, area, precision=HIGH) * hull_mask[None, None, :]
    )
    first_strengths = boundary.astype(jnp.bfloat16)
    kernel_scale = 1.0 / (4.0 * math.pi * math.sqrt(panels_total))
    own_geometry = jnp.concatenate([centroid, weight[:, None, :]], axis=1)
    sources = lax.all_gather(own_geometry, "panels", axis=2, tiled=True)
    row_targets = lax.all_gather(centroid, "cols", axis=2, tiled=True)

    def apply_influence(strengths):
        empty_sum = jnp.zeros((variant_dev, load_count, row_targets.shape[2]), jnp.float32)
        partial_sums = tile_product(
            empty_sum,
            row_targets,
            sources,
            lax.all_gather(strengths, "panels", axis=2, tiled=True),
            kernel_scale,
        )
        return lax.psum_scatter(partial_sums, "cols", scatter_dimension=2, tiled=True)

    induced = apply_influence(first_strengths)
    second_strengths = (first_strengths.astype(jnp.float32) + (boundary - induced)).astype(
        jnp.bfloat16
    )
    pressure = apply_influence(second_strengths)
    panel_force = pressure * (area[:, 2, :] * hull_mask[None, :])[:, None, :]
    force_rows = panel_force.reshape(-1, pan_dev)
    capacity = max(2, 5 * pan_dev // (2 * owners))
    target_owner = station_owner[:, 0]
    panel_order = jnp.arange(pan_dev, dtype=jnp.int32)
    ahead = (target_owner[:, None] == target_owner[None, :]) & (
        panel_order[None, :] < panel_order[:, None]
    )
    slot_rank = jnp.sum(ahead.astype(jnp.int32), axis=1)
    slot_index = target_owner * capacity + slot_rank
    all_slots = jnp.arange(owners * capacity, dtype=jnp.int32)
    placed = slot_index[:, None] == all_slots[None, :]
    send_values = jnp.dot(force_rows, placed.astype(jnp.float32), precision=HIGH)
    station_bins = (owner_index * pan_dev + panel_order) % STATIONS
    send_bins = jnp.max(jnp.where(placed, station_bins[:, None], -1), axis=0)[None, :]
    recv_values, recv_bins = (
        lax.all_to_all(send_values, ("panels", "cols"), split_axis=1, concat_axis=1, tiled=True),
        lax.all_to_all(send_bins, ("panels", "cols"), split_axis=1, concat_axis=1, tiled=True),
    )
    matches = (recv_bins[0][:, None] == jnp.arange(STATIONS, dtype=jnp.int32)[None, :]).astype(
        jnp.float32
    )
    station_loads = jnp.dot(recv_values, matches, precision=HIGH)
    station_place = (owner_index * STATIONS + jnp.arange(STATIONS, dtype=jnp.int32)).astype(
        jnp.float32
    ) / (STATIONS * owners)
    placed_loads = station_loads * station_place[None, :]
    own_total = jnp.sum(station_loads, axis=1)
    own_arm = jnp.sum(placed_loads, axis=1)
    zero_row = jnp.zeros_like(own_total)
    prior_total, prior_arm = prefix(
        (own_total, own_arm), ("panels", "cols"), add_pairs, (zero_row, zero_row)
    )
    station_rank = jnp.arange(STATIONS, dtype=jnp.int32)
    inclusive = (station_rank[:, None] <= station_rank[None, :]).astype(jnp.float32)
    strict = (station_rank[:, None] < station_rank[None, :]).astype(jnp.float32)
    running = prior_total[:, None] + jnp.dot(station_loads, inclusive, precision=HIGH)
    earlier = prior_total[:, None] + jnp.dot(station_loads, strict, precision=HIGH)
    moment_arm = prior_arm[:, None] + jnp.dot(placed_loads, strict, precision=HIGH)
    inv_root = 1.0 / math.sqrt(panels_total)
    shear = (running * inv_root).reshape(variant_dev, load_count, STATIONS)
    moment = ((station_place[None, :] * earlier - moment_arm) * inv_root).reshape(
        variant_dev, load_count, STATIONS
    )
    return (shear, moment)


TILE_ROWS = 8
HALF_ROWS = 4
LANES = 128
LOAD_GRANT = 16 << 20
FUSED_PANELS = 1024


def own_geometry_rows(weights, points_col, corner_rows, control_ref, vert_dev):
    controls = control_ref.shape[1]
    chunk = min(controls, 2 * LANES)
    totals = [jnp.zeros((vert_dev, chunk), jnp.float32) for _ in range(3)]
    columns = [jnp.broadcast_to(col, (vert_dev, chunk)) for col in points_col]
    for start in range(0, controls, chunk):
        span = slice(start, start + chunk)
        dx = control_ref[0:1, span] - columns[0]
        dy = control_ref[1:2, span] - columns[1]
        dz = control_ref[2:3, span] - columns[2]
        basis = lax.rsqrt(1.0 + (dx * dx + dy * dy + dz * dz))
        totals = [totals[a] + weights[a : a + 1, span] * basis for a in range(3)]
    moved = [points_col[a] + jnp.sum(totals[a], axis=1, keepdims=True) for a in range(3)]
    vertex = lax.broadcasted_iota(jnp.int32, (vert_dev, corner_rows.shape[1]), 0)
    corners = []
    for q in range(3):
        hit = vertex == corner_rows[q : q + 1, :]
        corners.append(
            [jnp.sum(jnp.where(hit, moved[a], 0.0), axis=0, keepdims=True) for a in range(3)]
        )
    p0, p1, p2 = corners
    centroid = [(p0[a] + p1[a] + p2[a]) / 3.0 for a in range(3)]
    e1 = [p1[a] - p0[a] for a in range(3)]
    e2 = [p2[a] - p0[a] for a in range(3)]
    area = [
        0.5 * (e1[1] * e2[2] - e1[2] * e2[1]),
        0.5 * (e1[2] * e2[0] - e1[0] * e2[2]),
        0.5 * (e1[0] * e2[1] - e1[1] * e2[0]),
    ]
    weight = jnp.sqrt(area[0] * area[0] + area[1] * area[1] + area[2] * area[2] + SKIN_SQUARE)
    return centroid, weight, area


def gather_kernel(
    panels_axis,
    cols_axis,
    order_hbm,
    base_hbm,
    control_hbm,
    morph_hbm,
    corner_hbm,
    flag_hbm,
    owner_hbm,
    velocity_hbm,
    gathered,
    influence_ref,
    order_ref,
    base_ref,
    control_ref,
    morph_ref,
    corner_ref,
    flag_ref,
    owner_ref,
    velocity_ref,
    mix_ref,
    spread_ref,
    in_sem,
    send_sem,
    recv_sem,
):
    owners = panels_axis * cols_axis
    row, col = lax.axis_index("panels"), lax.axis_index("cols")
    me = row * cols_axis + col
    vert_dev = base_ref.shape[1]
    pan_dev = corner_ref.shape[1]
    loads = velocity_ref.shape[1]
    panels_total = pan_dev * owners

    pairs = (
        (base_hbm, base_ref),
        (control_hbm, control_ref),
        (order_hbm, order_ref),
        (morph_hbm, morph_ref),
        (corner_hbm, corner_ref),
        (flag_hbm, flag_ref),
        (owner_hbm, owner_ref),
        (velocity_hbm, velocity_ref),
    )
    fetches = [
        pltpu.make_async_copy(source, target, in_sem.at[k])
        for k, (source, target) in enumerate(pairs)
    ]
    for fetch in fetches:
        fetch.start()
    steps = [(r, c) for r in range(panels_axis) for c in range(cols_axis)][::-1][:-1]
    peers = [
        {"panels": lax.rem(row + r, panels_axis), "cols": lax.rem(col + c, cols_axis)}
        for r, c in steps
    ]
    barrier = pltpu.get_barrier_semaphore()
    for peer in peers:
        pl.semaphore_signal(barrier, inc=1, device_id=peer, device_id_type=pl.DeviceIdType.MESH)
    mix_ref[...] = jnp.zeros(mix_ref.shape, jnp.float32)
    for fetch in fetches:
        fetch.wait()

    mix_ref[0:3, 0:vert_dev] = base_ref[...]
    mixed = mix_ref[...].T
    points_col = [mixed[0:vert_dev, a : a + 1] for a in range(3)]
    gathered[owners] = jnp.zeros((HALF_ROWS, LANES), jnp.float32)
    gathered[owners, 0:3, 0:loads] = velocity_ref[...]
    slot = order_ref[lax.axis_index("phase")]
    weights = jnp.concatenate([morph_ref[a, pl.ds(slot, 1), :] for a in range(3)], axis=0)
    centroid, weight, area = own_geometry_rows(
        weights, points_col, corner_ref[...] - me * vert_dev, control_ref, vert_dev
    )
    hull = (1 - flag_ref[...]).astype(jnp.float32)
    station = (
        owner_ref[...] * STATIONS
        + lax.rem(me * pan_dev, STATIONS)
        + lax.broadcasted_iota(jnp.int32, (1, pan_dev), 1)
    ).astype(jnp.float32)
    upper = jnp.concatenate(centroid + [weight], axis=0)
    lower = jnp.concatenate([part * hull for part in area] + [station], axis=0)
    gathered[me] = jnp.concatenate([upper, lower], axis=1)

    pl.semaphore_wait(barrier, owners - 1)
    sends = []
    for k, peer in enumerate(peers):
        send = pltpu.make_async_remote_copy(
            src_ref=gathered.at[me],
            dst_ref=gathered.at[me],
            send_sem=send_sem.at[k],
            recv_sem=recv_sem.at[me],
            device_id=peer,
            device_id_type=pl.DeviceIdType.MESH,
        )
        send.start()
        sends.append(send)

    kernel_scale = 1.0 / (4.0 * math.pi * math.sqrt(panels_total))
    tiles = panels_total // LANES
    per_tile = owners // tiles
    block = 32

    def fill(target_row, source_tile):
        for start in range(0, LANES, block):
            at = source_tile * LANES + start
            span = slice(at, at + block)
            dx = target_row[0:1] - spread_ref[0, span, :]
            dy = target_row[1:2] - spread_ref[1, span, :]
            dz = target_row[2:3] - spread_ref[2, span, :]
            distance = dx * dx + dy * dy + dz * dz
            yield span, (spread_ref[3, span, :] * lax.rsqrt(distance + CORE_SQUARE)).astype(
                jnp.bfloat16
            )

    tile_rows = []
    for tile in range(tiles):
        for source in range(tile * per_tile, (tile + 1) * per_tile):

            @pl.when(me != source)
            def _():
                pltpu.make_async_remote_copy(
                    src_ref=gathered.at[source],
                    dst_ref=gathered.at[source],
                    send_sem=send_sem.at[0],
                    recv_sem=recv_sem.at[source],
                    device_id=peers[0],
                    device_id_type=pl.DeviceIdType.MESH,
                ).wait_recv()

        own = jnp.concatenate(
            [gathered[tile * per_tile + d, :, 0:pan_dev] for d in range(per_tile)], axis=1
        )
        tile_rows.append(own)
        lanes = slice(tile * LANES, (tile + 1) * LANES)
        for before in range(tile):
            for span, value in fill(own, before):
                influence_ref[span, lanes] = value
        columns = jnp.concatenate([own, own], axis=0).T
        for a in range(4):
            column = columns[:, a : a + 1] * kernel_scale if a == 3 else columns[:, a : a + 1]
            spread_ref[a, lanes, :] = jnp.broadcast_to(column, (LANES, LANES))
        for target in range(tile + 1):
            for span, value in fill(tile_rows[target], tile):
                influence_ref[span, target * LANES : (target + 1) * LANES] = value
    for send in sends:
        send.wait_send()


def load_kernel(
    panels_axis, cols_axis, pan_dev, loads, gathered, influence_ref, shear_ref, moment_ref
):
    owners = panels_axis * cols_axis
    me = lax.axis_index("panels") * cols_axis + lax.axis_index("cols")
    panels_total = pan_dev * owners
    spread = jnp.concatenate([gathered[owners], gathered[owners]], axis=0).T
    velocity_col = [spread[0:loads, a : a + 1] for a in range(3)]
    rows = jnp.concatenate([gathered[d, :, pan_dev : 2 * pan_dev] for d in range(owners)], axis=1)
    columns = jnp.concatenate([rows, rows], axis=0).T
    boundary = (
        velocity_col[0] * rows[0:1] + velocity_col[1] * rows[1:2] + velocity_col[2] * rows[2:3]
    )
    first = boundary.astype(jnp.bfloat16)
    induced = jnp.dot(first, influence_ref[...], preferred_element_type=jnp.float32)
    second = (first.astype(jnp.float32) + (boundary - induced)).astype(jnp.bfloat16)
    pressure = jnp.dot(second, influence_ref[...], preferred_element_type=jnp.float32)
    force = pressure * rows[2:3]
    force_high = force.astype(jnp.bfloat16)
    force_low = (force - force_high.astype(jnp.float32)).astype(jnp.bfloat16)
    here = (
        me * STATIONS + lax.broadcasted_iota(jnp.int32, (panels_total, STATIONS), 1)
    ).astype(jnp.float32)
    gap = here - columns[:, 3:4]
    reached = jnp.where(gap >= 0.0, 1.0, 0.0).astype(jnp.bfloat16)
    arm = jnp.maximum(gap, 0.0)
    arm_high = arm.astype(jnp.bfloat16)
    arm_low = (arm - arm_high.astype(jnp.float32)).astype(jnp.bfloat16)
    summed = jnp.dot(
        jnp.concatenate([force_high, force_low], axis=0),
        jnp.concatenate([reached, arm_high, arm_low], axis=1),
        preferred_element_type=jnp.float32,
    )
    summed = summed[0:loads] + summed[loads : 2 * loads]
    inv_root = 1.0 / math.sqrt(panels_total)
    shear_ref[0] = summed[:, 0:STATIONS] * inv_root
    moment_ref[0] = (summed[:, STATIONS : 2 * STATIONS] + summed[:, 2 * STATIONS :]) * (
        inv_root / (STATIONS * owners)
    )


def fused_shards(
    panels_axis,
    cols_axis,
    base_points,
    control_points,
    morph_weights,
    connectivity,
    free_flags,
    station_owner,
    variant_order,
    load_velocity,
):
    owners = panels_axis * cols_axis
    pan_dev = connectivity.shape[1]
    loads = load_velocity.shape[0]
    panels_total = pan_dev * owners
    hbm_inputs = (
        variant_order,
        base_points,
        control_points,
        morph_weights.transpose(1, 0, 2),
        connectivity,
        free_flags.reshape(1, pan_dev),
        station_owner.reshape(1, pan_dev),
        load_velocity.T,
    )
    gathered, influence = pl.pallas_call(
        functools.partial(gather_kernel, panels_axis, cols_axis),
        out_shape=(
            pltpu.VMEM((owners + 1, HALF_ROWS, LANES), jnp.float32),
            pltpu.VMEM((panels_total, panels_total), jnp.bfloat16),
        ),
        in_specs=[pl.BlockSpec(memory_space=pltpu.HBM)] * len(hbm_inputs),
        out_specs=(pl.BlockSpec(memory_space=pltpu.VMEM),) * 2,
        scratch_shapes=[pltpu.SMEM(variant_order.shape, variant_order.dtype)]
        + [pltpu.VMEM(part.shape, part.dtype) for part in hbm_inputs[1:]]
        + [
            pltpu.VMEM((TILE_ROWS, LANES), jnp.float32),
            pltpu.VMEM((HALF_ROWS, panels_total, LANES), jnp.float32),
            pltpu.SemaphoreType.DMA((len(hbm_inputs),)),
            pltpu.SemaphoreType.DMA((owners,)),
            pltpu.SemaphoreType.DMA((owners,)),
        ],
        compiler_params=pltpu.CompilerParams(
            collective_id=0, has_side_effects=True
        ),
    )(*hbm_inputs)
    result = jax.ShapeDtypeStruct((1, loads, STATIONS), jnp.float32)
    return tuple(
        pl.pallas_call(
            functools.partial(load_kernel, panels_axis, cols_axis, pan_dev, loads),
            out_shape=(result, result),
            in_specs=[pl.BlockSpec(memory_space=pltpu.VMEM)] * 2,
            out_specs=(pl.BlockSpec(memory_space=pltpu.VMEM),) * 2,
            compiler_params=pltpu.CompilerParams(vmem_limit_bytes=LOAD_GRANT),
        )(gathered, influence)
    )


def choose_shards(mesh, *arrays):
    panels_axis, cols_axis = mesh.shape["panels"], mesh.shape["cols"]
    owners = panels_axis * cols_axis
    base_points, connectivity, variant_order, load_velocity = (
        arrays[0],
        arrays[3],
        arrays[6],
        arrays[7],
    )
    pan_dev = connectivity.shape[1]
    fits = (
        pan_dev * owners <= FUSED_PANELS
        and LANES == 2 * pan_dev
        and STATIONS % pan_dev == 0
        and owners % 2 == 0
        and base_points.shape[1] <= LANES
        and load_velocity.shape[0] <= LANES
        and variant_order.shape[0] == mesh.shape["phase"]
    )
    if fits:
        return fused_shards(panels_axis, cols_axis, *arrays)
    return shards(*arrays)


def solution(mesh):
    return jax.shard_map(
        functools.partial(choose_shards, mesh),
        mesh=mesh,
        in_specs=(
            P(None, ("groups", "panels", "cols")),
            P(),
            P("groups", None, None),
            P(None, ("groups", "panels", "cols")),
            P(("groups", "panels", "cols")),
            P(("groups", "panels", "cols"), None),
            P("groups"),
            P(),
        ),
        out_specs=(
            P(("groups", "phase"), None, ("panels", "cols")),
            P(("groups", "phase"), None, ("panels", "cols")),
        ),
        check_vma=False,
    )
```

```python
import functools
import math

import jax
import jax.numpy as jnp
from jax import lax
from jax.experimental import pallas as pl
from jax.experimental.pallas import tpu as pltpu
from jax.sharding import PartitionSpec as P

STATIONS = 128


HIGH = lax.Precision.HIGHEST
CORE_SQUARE = 0.0025
SKIN_SQUARE = 0.01


def prefix(shard, axis, combine, identity):
    length, index = (lax.axis_size(axis), lax.axis_index(axis))
    everything = jax.tree.map(lambda part: lax.all_gather(part, axis), shard)
    start = jax.tree.map(
        lambda part, zero: jnp.broadcast_to(jnp.asarray(zero, part.dtype), part.shape),
        shard,
        identity,
    )

    def step(k, before):
        reached = k < index
        new = combine(before, jax.tree.map(lambda part: part[k], everything))
        return jax.tree.map(lambda a, b: jnp.where(reached, a, b), new, before)

    return lax.fori_loop(0, length, step, start)


def panel_shape(moved_points, corner_rows):
    first_corner = jnp.take(moved_points, corner_rows[0], axis=2)
    second_corner = jnp.take(moved_points, corner_rows[1], axis=2)
    third_corner = jnp.take(moved_points, corner_rows[2], axis=2)
    centroid = (first_corner + second_corner + third_corner) / 3.0
    edge_one = second_corner - first_corner
    edge_two = third_corner - first_corner
    cross_x = edge_one[:, 1] * edge_two[:, 2] - edge_one[:, 2] * edge_two[:, 1]
    cross_y = edge_one[:, 2] * edge_two[:, 0] - edge_one[:, 0] * edge_two[:, 2]
    cross_z = edge_one[:, 0] * edge_two[:, 1] - edge_one[:, 1] * edge_two[:, 0]
    area = 0.5 * jnp.stack([cross_x, cross_y, cross_z], axis=1)
    weight = jnp.sqrt(jnp.sum(area * area, axis=1) + SKIN_SQUARE)
    return (centroid, area, weight)


def tile_block(targets, sources, strengths, kernel_scale):
    distance = (
        (targets[:, 0, :, None] - sources[:, 0, None, :]) ** 2
        + (targets[:, 1, :, None] - sources[:, 1, None, :]) ** 2
        + (targets[:, 2, :, None] - sources[:, 2, None, :]) ** 2
    )
    influence = (sources[:, 3, None, :] * kernel_scale * lax.rsqrt(distance + CORE_SQUARE)).astype(
        jnp.bfloat16
    )
    return jnp.einsum("mrn,mkn->mkr", influence, strengths, preferred_element_type=jnp.float32)


def tile_product(carry_sum, targets, sources, strengths, kernel_scale):
    columns = strengths.shape[2]
    block_width = columns
    for candidate in (2048, 1024, 512):
        if columns > candidate and columns % candidate == 0:
            block_width = candidate
            break
    if block_width == columns:
        return carry_sum + tile_block(targets, sources, strengths, kernel_scale)

    def block_step(step_index, running_sum):
        column_start = step_index * block_width
        part_sources = lax.dynamic_slice_in_dim(sources, column_start, block_width, 2)
        part_strengths = lax.dynamic_slice_in_dim(strengths, column_start, block_width, 2)
        return running_sum + tile_block(targets, part_sources, part_strengths, kernel_scale)

    return lax.fori_loop(0, columns // block_width, block_step, carry_sum)


def add_pairs(earlier, later):
    return (earlier[0] + later[0], earlier[1] + later[1])


def shards(
    base_points,
    control_points,
    morph_weights,
    connectivity,
    free_flags,
    station_owner,
    variant_order,
    load_velocity,
):
    owners = lax.axis_size(("panels", "cols"))
    owner_index = lax.axis_index(("panels", "cols"))
    phase_index = lax.axis_index("phase")
    variant_dev = variant_order.shape[0] // lax.axis_size("phase")
    vert_dev = base_points.shape[1]
    pan_dev = connectivity.shape[1]
    load_count = load_velocity.shape[0]
    panels_total = pan_dev * owners
    own_variants = lax.dynamic_slice_in_dim(
        variant_order, phase_index * variant_dev, variant_dev, 0
    )
    picker = (
        own_variants[:, None] == jnp.arange(variant_order.shape[0], dtype=jnp.int32)[None, :]
    ).astype(jnp.float32)
    chosen = jnp.einsum("mv,vac->mac", picker, morph_weights, precision=HIGH)
    distance = (
        (control_points[0][:, None] - base_points[0][None, :]) ** 2
        + (control_points[1][:, None] - base_points[1][None, :]) ** 2
        + (control_points[2][:, None] - base_points[2][None, :]) ** 2
    )
    basis_values = lax.rsqrt(1.0 + distance)
    moved_points = base_points[None] + jnp.einsum(
        "mac,cn->man", chosen, basis_values, precision=HIGH
    )
    local_corners = connectivity - owner_index * vert_dev
    centroid, area, weight = panel_shape(moved_points, local_corners)
    hull_mask = (1 - free_flags).astype(jnp.float32)
    boundary = (
        jnp.einsum("ka,man->mkn", load_velocity, area, precision=HIGH) * hull_mask[None, None, :]
    )
    first_strengths = boundary.astype(jnp.bfloat16)
    kernel_scale = 1.0 / (4.0 * math.pi * math.sqrt(panels_total))
    own_geometry = jnp.concatenate([centroid, weight[:, None, :]], axis=1)
    sources = lax.all_gather(own_geometry, "panels", axis=2, tiled=True)
    row_targets = lax.all_gather(centroid, "cols", axis=2, tiled=True)

    def apply_influence(strengths):
        empty_sum = jnp.zeros((variant_dev, load_count, row_targets.shape[2]), jnp.float32)
        partial_sums = tile_product(
            empty_sum,
            row_targets,
            sources,
            lax.all_gather(strengths, "panels", axis=2, tiled=True),
            kernel_scale,
        )
        return lax.psum_scatter(partial_sums, "cols", scatter_dimension=2, tiled=True)

    induced = apply_influence(first_strengths)
    second_strengths = (first_strengths.astype(jnp.float32) + (boundary - induced)).astype(
        jnp.bfloat16
    )
    pressure = apply_influence(second_strengths)
    panel_force = pressure * (area[:, 2, :] * hull_mask[None, :])[:, None, :]
    force_rows = panel_force.reshape(-1, pan_dev)
    capacity = max(2, 5 * pan_dev // (2 * owners))
    target_owner = station_owner[:, 0]
    panel_order = jnp.arange(pan_dev, dtype=jnp.int32)
    ahead = (target_owner[:, None] == target_owner[None, :]) & (
        panel_order[None, :] < panel_order[:, None]
    )
    slot_rank = jnp.sum(ahead.astype(jnp.int32), axis=1)
    slot_index = target_owner * capacity + slot_rank
    all_slots = jnp.arange(owners * capacity, dtype=jnp.int32)
    placed = slot_index[:, None] == all_slots[None, :]
    send_values = jnp.dot(force_rows, placed.astype(jnp.float32), precision=HIGH)
    station_bins = (owner_index * pan_dev + panel_order) % STATIONS
    send_bins = jnp.max(jnp.where(placed, station_bins[:, None], -1), axis=0)[None, :]
    recv_values, recv_bins = (
        lax.all_to_all(send_values, ("panels", "cols"), split_axis=1, concat_axis=1, tiled=True),
        lax.all_to_all(send_bins, ("panels", "cols"), split_axis=1, concat_axis=1, tiled=True),
    )
    matches = (recv_bins[0][:, None] == jnp.arange(STATIONS, dtype=jnp.int32)[None, :]).astype(
        jnp.float32
    )
    station_loads = jnp.dot(recv_values, matches, precision=HIGH)
    station_place = (owner_index * STATIONS + jnp.arange(STATIONS, dtype=jnp.int32)).astype(
        jnp.float32
    ) / (STATIONS * owners)
    placed_loads = station_loads * station_place[None, :]
    own_total = jnp.sum(station_loads, axis=1)
    own_arm = jnp.sum(placed_loads, axis=1)
    zero_row = jnp.zeros_like(own_total)
    prior_total, prior_arm = prefix(
        (own_total, own_arm), ("panels", "cols"), add_pairs, (zero_row, zero_row)
    )
    station_rank = jnp.arange(STATIONS, dtype=jnp.int32)
    inclusive = (station_rank[:, None] <= station_rank[None, :]).astype(jnp.float32)
    strict = (station_rank[:, None] < station_rank[None, :]).astype(jnp.float32)
    running = prior_total[:, None] + jnp.dot(station_loads, inclusive, precision=HIGH)
    earlier = prior_total[:, None] + jnp.dot(station_loads, strict, precision=HIGH)
    moment_arm = prior_arm[:, None] + jnp.dot(placed_loads, strict, precision=HIGH)
    inv_root = 1.0 / math.sqrt(panels_total)
    shear = (running * inv_root).reshape(variant_dev, load_count, STATIONS)
    moment = ((station_place[None, :] * earlier - moment_arm) * inv_root).reshape(
        variant_dev, load_count, STATIONS
    )
    return (shear, moment)


TILE_ROWS = 8
HALF_ROWS = 4
LANES = 128
LOAD_GRANT = 16 << 20
FUSED_PANELS = 1024


def own_geometry_rows(weights_of, points_col, corner_rows_of, control_ref, vert_dev, before_chunk):
    controls = control_ref.shape[1]
    chunk = min(controls, 2 * LANES)
    totals = [jnp.zeros((vert_dev, chunk), jnp.float32) for _ in range(3)]
    columns = [jnp.broadcast_to(col, (vert_dev, chunk)) for col in points_col]
    for start in range(0, controls, chunk):
        span = slice(start, start + chunk)
        before_chunk(start)
        weights = weights_of(span)
        dx = control_ref[0:1, span] - columns[0]
        dy = control_ref[1:2, span] - columns[1]
        dz = control_ref[2:3, span] - columns[2]
        basis = lax.rsqrt(1.0 + (dx * dx + dy * dy + dz * dz))
        totals = [totals[a] + weights[a] * basis for a in range(3)]
    moved = [points_col[a] + jnp.sum(totals[a], axis=1, keepdims=True) for a in range(3)]
    corner_rows = corner_rows_of()
    vertex = lax.broadcasted_iota(jnp.int32, (vert_dev, corner_rows.shape[1]), 0)
    corners = []
    for q in range(3):
        hit = vertex == corner_rows[q : q + 1, :]
        corners.append(
            [jnp.sum(jnp.where(hit, moved[a], 0.0), axis=0, keepdims=True) for a in range(3)]
        )
    p0, p1, p2 = corners
    centroid = [(p0[a] + p1[a] + p2[a]) / 3.0 for a in range(3)]
    e1 = [p1[a] - p0[a] for a in range(3)]
    e2 = [p2[a] - p0[a] for a in range(3)]
    area = [
        0.5 * (e1[1] * e2[2] - e1[2] * e2[1]),
        0.5 * (e1[2] * e2[0] - e1[0] * e2[2]),
        0.5 * (e1[0] * e2[1] - e1[1] * e2[0]),
    ]
    weight = jnp.sqrt(area[0] * area[0] + area[1] * area[1] + area[2] * area[2] + SKIN_SQUARE)
    return centroid, weight, area


def gather_kernel(
    panels_axis,
    cols_axis,
    order_hbm,
    base_hbm,
    control_hbm,
    morph_hbm,
    corner_hbm,
    flag_hbm,
    owner_hbm,
    velocity_hbm,
    influence_ref,
    masks_ref,
    boundary_ref,
    lift_ref,
    order_ref,
    base_ref,
    control_ref,
    morph_ref,
    corner_ref,
    flag_ref,
    owner_ref,
    velocity_ref,
    mix_ref,
    spread_ref,
    gathered,
    in_sem,
    send_sem,
    recv_sem,
):
    owners = panels_axis * cols_axis
    row, col = lax.axis_index("panels"), lax.axis_index("cols")
    me = row * cols_axis + col
    vert_dev = base_ref.shape[1]
    pan_dev = corner_ref.shape[1]
    loads = velocity_ref.shape[1]
    panels_total = pan_dev * owners

    halves = 2
    wide = control_ref.shape[1] // halves
    pairs = [(base_hbm, base_ref), (order_hbm, order_ref)]
    for half in range(halves):
        span = pl.ds(half * wide, wide)
        pairs += [
            (control_hbm.at[:, span], control_ref.at[:, span]),
            (morph_hbm.at[:, :, span], morph_ref.at[:, :, span]),
        ]
    pairs += [
        (corner_hbm, corner_ref),
        (flag_hbm, flag_ref),
        (owner_hbm, owner_ref),
        (velocity_hbm, velocity_ref),
    ]
    fetches = [
        pltpu.make_async_copy(source, target, in_sem.at[k])
        for k, (source, target) in enumerate(pairs)
    ]
    for fetch in fetches:
        fetch.start()
    steps = [
        (r % panels_axis, c)
        for r in range(1, panels_axis + 1)
        for c in reversed(range(cols_axis))
    ][:-1]
    peers = [
        {"panels": lax.rem(row + r, panels_axis), "cols": lax.rem(col + c, cols_axis)}
        for r, c in steps
    ]
    barrier = pltpu.get_barrier_semaphore()
    for peer in peers:
        pl.semaphore_signal(barrier, inc=1, device_id=peer, device_id_type=pl.DeviceIdType.MESH)
    mix_ref[...] = jnp.zeros(mix_ref.shape, jnp.float32)
    fetches[0].wait()
    mix_ref[0:3, 0:vert_dev] = base_ref[...]
    mixed = mix_ref[...].T
    points_col = [mixed[0:vert_dev, a : a + 1] for a in range(3)]
    fetches[1].wait()
    slot = order_ref[lax.axis_index("phase")]

    def before_chunk(start):
        if start % wide == 0:
            for part in range(2):
                fetches[2 + 2 * (start // wide) + part].wait()

    def weights_of(span):
        picked = [morph_ref[a, 0:1, span] for a in range(3)]
        for v in range(1, morph_ref.shape[1]):
            other = [morph_ref[a, v : v + 1, span] for a in range(3)]
            picked = [jnp.where(slot == v, new, old) for new, old in zip(other, picked)]
        return picked

    def corner_rows_of():
        for fetch in fetches[-4:]:
            fetch.wait()
        return corner_ref[...] - me * vert_dev

    centroid, weight, area = own_geometry_rows(
        weights_of,
        points_col,
        corner_rows_of,
        control_ref,
        vert_dev,
        before_chunk,
    )
    hull = (1 - flag_ref[...]).astype(jnp.float32)
    station = (
        owner_ref[...] * STATIONS
        + lax.rem(me * pan_dev, STATIONS)
        + lax.broadcasted_iota(jnp.int32, (1, pan_dev), 1)
    ).astype(jnp.float32)
    upper = jnp.concatenate(centroid + [weight], axis=0)
    lower = jnp.concatenate([part * hull for part in area] + [station], axis=0)
    gathered[me] = jnp.concatenate([upper, lower], axis=1)

    pl.semaphore_wait(barrier, owners - 1)
    sends = []
    for k, peer in enumerate(peers):
        send = pltpu.make_async_remote_copy(
            src_ref=gathered.at[me],
            dst_ref=gathered.at[me],
            send_sem=send_sem.at[k],
            recv_sem=recv_sem.at[me],
            device_id=peer,
            device_id_type=pl.DeviceIdType.MESH,
        )
        send.start()
        sends.append(send)

    mix_ref[0:3, 0:loads] = velocity_ref[...]
    velocity = mix_ref[...].T
    velocity_col = [velocity[0:loads, a : a + 1] for a in range(3)]
    here = (me * STATIONS + lax.broadcasted_iota(jnp.int32, (LANES, STATIONS), 1)).astype(
        jnp.float32
    )
    kernel_scale = 1.0 / (4.0 * math.pi * math.sqrt(panels_total))
    tiles = panels_total // LANES
    per_tile = owners // tiles
    block = 32

    def fill(target_row, source_tile):
        for start in range(0, LANES, block):
            at = source_tile * LANES + start
            span = slice(at, at + block)
            dx = target_row[0:1] - spread_ref[0, span, :]
            dy = target_row[1:2] - spread_ref[1, span, :]
            dz = target_row[2:3] - spread_ref[2, span, :]
            distance = dx * dx + dy * dy + dz * dz
            yield span, (spread_ref[3, span, :] * lax.rsqrt(distance + CORE_SQUARE)).astype(
                jnp.bfloat16
            )

    tile_rows = []
    for tile in range(tiles):
        for source in range(tile * per_tile, (tile + 1) * per_tile):

            @pl.when(me != source)
            def _():
                pltpu.make_async_remote_copy(
                    src_ref=gathered.at[source],
                    dst_ref=gathered.at[source],
                    send_sem=send_sem.at[0],
                    recv_sem=recv_sem.at[source],
                    device_id=peers[0],
                    device_id_type=pl.DeviceIdType.MESH,
                ).wait_recv()

        blocks = [gathered[tile * per_tile + d] for d in range(per_tile)]
        own = jnp.concatenate([part[:, 0:pan_dev] for part in blocks], axis=1)
        load = jnp.concatenate([part[:, pan_dev : 2 * pan_dev] for part in blocks], axis=1)
        tile_rows.append(own)
        columns = jnp.concatenate([own, load], axis=0).T
        lanes = slice(tile * LANES, (tile + 1) * LANES)
        boundary_ref[:, lanes] = (
            velocity_col[0] * load[0:1] + velocity_col[1] * load[1:2] + velocity_col[2] * load[2:3]
        )
        lift_ref[:, lanes] = load[2:3]
        for before in range(tile):
            for span, value in fill(own, before):
                influence_ref[span, lanes] = value
        for a in range(4):
            column = columns[:, a : a + 1] * kernel_scale if a == 3 else columns[:, a : a + 1]
            spread_ref[a, lanes, :] = jnp.broadcast_to(column, (LANES, LANES))
        for target in range(tile + 1):
            for span, value in fill(tile_rows[target], tile):
                influence_ref[span, target * LANES : (target + 1) * LANES] = value
        gap = here - columns[:, 7:8]
        arm = jnp.maximum(gap, 0.0)
        arm_high = arm.astype(jnp.bfloat16)
        masks_ref[lanes, 0:STATIONS] = jnp.where(gap >= 0.0, 1.0, 0.0).astype(jnp.bfloat16)
        masks_ref[lanes, STATIONS : 2 * STATIONS] = arm_high
        masks_ref[lanes, 2 * STATIONS :] = (arm - arm_high.astype(jnp.float32)).astype(
            jnp.bfloat16
        )
    for send in sends:
        send.wait_send()


def load_kernel(owners, influence_ref, masks_ref, boundary_ref, lift_ref, shear_ref, moment_ref):
    loads, panels_total = boundary_ref.shape
    boundary = boundary_ref[...]
    first = boundary.astype(jnp.bfloat16)
    induced = jnp.dot(first, influence_ref[...], preferred_element_type=jnp.float32)
    second = (first.astype(jnp.float32) + (boundary - induced)).astype(jnp.bfloat16)
    pressure = jnp.dot(second, influence_ref[...], preferred_element_type=jnp.float32)
    force = pressure * lift_ref[...]
    force_high = force.astype(jnp.bfloat16)
    force_low = (force - force_high.astype(jnp.float32)).astype(jnp.bfloat16)
    summed = jnp.dot(
        jnp.concatenate([force_high, force_low], axis=0),
        masks_ref[...],
        preferred_element_type=jnp.float32,
    )
    summed = summed[0:loads] + summed[loads : 2 * loads]
    inv_root = 1.0 / math.sqrt(panels_total)
    shear_ref[0] = summed[:, 0:STATIONS] * inv_root
    moment_ref[0] = (summed[:, STATIONS : 2 * STATIONS] + summed[:, 2 * STATIONS :]) * (
        inv_root / (STATIONS * owners)
    )


def fused_shards(
    panels_axis,
    cols_axis,
    base_points,
    control_points,
    morph_weights,
    connectivity,
    free_flags,
    station_owner,
    variant_order,
    load_velocity,
):
    owners = panels_axis * cols_axis
    pan_dev = connectivity.shape[1]
    loads = load_velocity.shape[0]
    panels_total = pan_dev * owners
    hbm_inputs = (
        variant_order,
        base_points,
        control_points,
        morph_weights.transpose(1, 0, 2),
        connectivity,
        free_flags.reshape(1, pan_dev),
        station_owner.reshape(1, pan_dev),
        load_velocity.T,
    )
    parts = pl.pallas_call(
        functools.partial(gather_kernel, panels_axis, cols_axis),
        out_shape=(
            pltpu.VMEM((panels_total, panels_total), jnp.bfloat16),
            pltpu.VMEM((panels_total, 3 * STATIONS), jnp.bfloat16),
            pltpu.VMEM((loads, panels_total), jnp.float32),
            pltpu.VMEM((1, panels_total), jnp.float32),
        ),
        in_specs=[pl.BlockSpec(memory_space=pltpu.HBM)] * len(hbm_inputs),
        out_specs=(pl.BlockSpec(memory_space=pltpu.VMEM),) * 4,
        scratch_shapes=[pltpu.SMEM(variant_order.shape, variant_order.dtype)]
        + [pltpu.VMEM(part.shape, part.dtype) for part in hbm_inputs[1:]]
        + [
            pltpu.VMEM((TILE_ROWS, LANES), jnp.float32),
            pltpu.VMEM((HALF_ROWS, panels_total, LANES), jnp.float32),
            pltpu.VMEM((owners, HALF_ROWS, LANES), jnp.float32),
            pltpu.SemaphoreType.DMA((len(hbm_inputs) + 2,)),
            pltpu.SemaphoreType.DMA((owners,)),
            pltpu.SemaphoreType.DMA((owners,)),
        ],
        compiler_params=pltpu.CompilerParams(
            collective_id=0, has_side_effects=True
        ),
    )(*hbm_inputs)
    result = jax.ShapeDtypeStruct((1, loads, STATIONS), jnp.float32)
    return tuple(
        pl.pallas_call(
            functools.partial(load_kernel, owners),
            out_shape=(result, result),
            in_specs=[pl.BlockSpec(memory_space=pltpu.VMEM)] * 4,
            out_specs=(pl.BlockSpec(memory_space=pltpu.VMEM),) * 2,
            compiler_params=pltpu.CompilerParams(vmem_limit_bytes=LOAD_GRANT),
        )(*parts)
    )


def choose_shards(mesh, *arrays):
    panels_axis, cols_axis = mesh.shape["panels"], mesh.shape["cols"]
    owners = panels_axis * cols_axis
    base_points, connectivity, variant_order, load_velocity = (
        arrays[0],
        arrays[3],
        arrays[6],
        arrays[7],
    )
    pan_dev = connectivity.shape[1]
    fits = (
        pan_dev * owners <= FUSED_PANELS
        and LANES == 2 * pan_dev
        and STATIONS % pan_dev == 0
        and owners % 2 == 0
        and base_points.shape[1] <= LANES
        and load_velocity.shape[0] <= LANES
        and variant_order.shape[0] == mesh.shape["phase"]
    )
    if fits:
        return fused_shards(panels_axis, cols_axis, *arrays)
    return shards(*arrays)


def solution(mesh):
    return jax.shard_map(
        functools.partial(choose_shards, mesh),
        mesh=mesh,
        in_specs=(
            P(None, ("groups", "panels", "cols")),
            P(),
            P("groups", None, None),
            P(None, ("groups", "panels", "cols")),
            P(("groups", "panels", "cols")),
            P(("groups", "panels", "cols"), None),
            P("groups"),
            P(),
        ),
        out_specs=(
            P(("groups", "phase"), None, ("panels", "cols")),
            P(("groups", "phase"), None, ("panels", "cols")),
        ),
        check_vma=False,
    )
```

```python
import functools
import math

import jax
import jax.numpy as jnp
from jax import lax
from jax.experimental import pallas as pl
from jax.experimental.pallas import tpu as pltpu
from jax.sharding import PartitionSpec as P

STATIONS = 128


HIGH = lax.Precision.HIGHEST
CORE_SQUARE = 0.0025
SKIN_SQUARE = 0.01


def prefix(shard, axis, combine, identity):
    length, index = (lax.axis_size(axis), lax.axis_index(axis))
    everything = jax.tree.map(lambda part: lax.all_gather(part, axis), shard)
    start = jax.tree.map(
        lambda part, zero: jnp.broadcast_to(jnp.asarray(zero, part.dtype), part.shape),
        shard,
        identity,
    )

    def step(k, before):
        reached = k < index
        new = combine(before, jax.tree.map(lambda part: part[k], everything))
        return jax.tree.map(lambda a, b: jnp.where(reached, a, b), new, before)

    return lax.fori_loop(0, length, step, start)


def panel_shape(moved_points, corner_rows):
    first_corner = jnp.take(moved_points, corner_rows[0], axis=2)
    second_corner = jnp.take(moved_points, corner_rows[1], axis=2)
    third_corner = jnp.take(moved_points, corner_rows[2], axis=2)
    centroid = (first_corner + second_corner + third_corner) / 3.0
    edge_one = second_corner - first_corner
    edge_two = third_corner - first_corner
    cross_x = edge_one[:, 1] * edge_two[:, 2] - edge_one[:, 2] * edge_two[:, 1]
    cross_y = edge_one[:, 2] * edge_two[:, 0] - edge_one[:, 0] * edge_two[:, 2]
    cross_z = edge_one[:, 0] * edge_two[:, 1] - edge_one[:, 1] * edge_two[:, 0]
    area = 0.5 * jnp.stack([cross_x, cross_y, cross_z], axis=1)
    weight = jnp.sqrt(jnp.sum(area * area, axis=1) + SKIN_SQUARE)
    return (centroid, area, weight)


def tile_block(targets, sources, strengths, kernel_scale):
    distance = (
        (targets[:, 0, :, None] - sources[:, 0, None, :]) ** 2
        + (targets[:, 1, :, None] - sources[:, 1, None, :]) ** 2
        + (targets[:, 2, :, None] - sources[:, 2, None, :]) ** 2
    )
    influence = (sources[:, 3, None, :] * kernel_scale * lax.rsqrt(distance + CORE_SQUARE)).astype(
        jnp.bfloat16
    )
    return jnp.einsum("mrn,mkn->mkr", influence, strengths, preferred_element_type=jnp.float32)


def tile_product(carry_sum, targets, sources, strengths, kernel_scale):
    columns = strengths.shape[2]
    block_width = columns
    for candidate in (2048, 1024, 512):
        if columns > candidate and columns % candidate == 0:
            block_width = candidate
            break
    if block_width == columns:
        return carry_sum + tile_block(targets, sources, strengths, kernel_scale)

    def block_step(step_index, running_sum):
        column_start = step_index * block_width
        part_sources = lax.dynamic_slice_in_dim(sources, column_start, block_width, 2)
        part_strengths = lax.dynamic_slice_in_dim(strengths, column_start, block_width, 2)
        return running_sum + tile_block(targets, part_sources, part_strengths, kernel_scale)

    return lax.fori_loop(0, columns // block_width, block_step, carry_sum)


def add_pairs(earlier, later):
    return (earlier[0] + later[0], earlier[1] + later[1])


def shards(
    base_points,
    control_points,
    morph_weights,
    connectivity,
    free_flags,
    station_owner,
    variant_order,
    load_velocity,
):
    owners = lax.axis_size(("panels", "cols"))
    owner_index = lax.axis_index(("panels", "cols"))
    phase_index = lax.axis_index("phase")
    variant_dev = variant_order.shape[0] // lax.axis_size("phase")
    vert_dev = base_points.shape[1]
    pan_dev = connectivity.shape[1]
    load_count = load_velocity.shape[0]
    panels_total = pan_dev * owners
    own_variants = lax.dynamic_slice_in_dim(
        variant_order, phase_index * variant_dev, variant_dev, 0
    )
    picker = (
        own_variants[:, None] == jnp.arange(variant_order.shape[0], dtype=jnp.int32)[None, :]
    ).astype(jnp.float32)
    chosen = jnp.einsum("mv,vac->mac", picker, morph_weights, precision=HIGH)
    distance = (
        (control_points[0][:, None] - base_points[0][None, :]) ** 2
        + (control_points[1][:, None] - base_points[1][None, :]) ** 2
        + (control_points[2][:, None] - base_points[2][None, :]) ** 2
    )
    basis_values = lax.rsqrt(1.0 + distance)
    moved_points = base_points[None] + jnp.einsum(
        "mac,cn->man", chosen, basis_values, precision=HIGH
    )
    local_corners = connectivity - owner_index * vert_dev
    centroid, area, weight = panel_shape(moved_points, local_corners)
    hull_mask = (1 - free_flags).astype(jnp.float32)
    boundary = (
        jnp.einsum("ka,man->mkn", load_velocity, area, precision=HIGH) * hull_mask[None, None, :]
    )
    first_strengths = boundary.astype(jnp.bfloat16)
    kernel_scale = 1.0 / (4.0 * math.pi * math.sqrt(panels_total))
    own_geometry = jnp.concatenate([centroid, weight[:, None, :]], axis=1)
    sources = lax.all_gather(own_geometry, "panels", axis=2, tiled=True)
    row_targets = lax.all_gather(centroid, "cols", axis=2, tiled=True)

    def apply_influence(strengths):
        empty_sum = jnp.zeros((variant_dev, load_count, row_targets.shape[2]), jnp.float32)
        partial_sums = tile_product(
            empty_sum,
            row_targets,
            sources,
            lax.all_gather(strengths, "panels", axis=2, tiled=True),
            kernel_scale,
        )
        return lax.psum_scatter(partial_sums, "cols", scatter_dimension=2, tiled=True)

    induced = apply_influence(first_strengths)
    second_strengths = (first_strengths.astype(jnp.float32) + (boundary - induced)).astype(
        jnp.bfloat16
    )
    pressure = apply_influence(second_strengths)
    panel_force = pressure * (area[:, 2, :] * hull_mask[None, :])[:, None, :]
    force_rows = panel_force.reshape(-1, pan_dev)
    capacity = max(2, 5 * pan_dev // (2 * owners))
    target_owner = station_owner[:, 0]
    panel_order = jnp.arange(pan_dev, dtype=jnp.int32)
    ahead = (target_owner[:, None] == target_owner[None, :]) & (
        panel_order[None, :] < panel_order[:, None]
    )
    slot_rank = jnp.sum(ahead.astype(jnp.int32), axis=1)
    slot_index = target_owner * capacity + slot_rank
    all_slots = jnp.arange(owners * capacity, dtype=jnp.int32)
    placed = slot_index[:, None] == all_slots[None, :]
    send_values = jnp.dot(force_rows, placed.astype(jnp.float32), precision=HIGH)
    station_bins = (owner_index * pan_dev + panel_order) % STATIONS
    send_bins = jnp.max(jnp.where(placed, station_bins[:, None], -1), axis=0)[None, :]
    recv_values, recv_bins = (
        lax.all_to_all(send_values, ("panels", "cols"), split_axis=1, concat_axis=1, tiled=True),
        lax.all_to_all(send_bins, ("panels", "cols"), split_axis=1, concat_axis=1, tiled=True),
    )
    matches = (recv_bins[0][:, None] == jnp.arange(STATIONS, dtype=jnp.int32)[None, :]).astype(
        jnp.float32
    )
    station_loads = jnp.dot(recv_values, matches, precision=HIGH)
    station_place = (owner_index * STATIONS + jnp.arange(STATIONS, dtype=jnp.int32)).astype(
        jnp.float32
    ) / (STATIONS * owners)
    placed_loads = station_loads * station_place[None, :]
    own_total = jnp.sum(station_loads, axis=1)
    own_arm = jnp.sum(placed_loads, axis=1)
    zero_row = jnp.zeros_like(own_total)
    prior_total, prior_arm = prefix(
        (own_total, own_arm), ("panels", "cols"), add_pairs, (zero_row, zero_row)
    )
    station_rank = jnp.arange(STATIONS, dtype=jnp.int32)
    inclusive = (station_rank[:, None] <= station_rank[None, :]).astype(jnp.float32)
    strict = (station_rank[:, None] < station_rank[None, :]).astype(jnp.float32)
    running = prior_total[:, None] + jnp.dot(station_loads, inclusive, precision=HIGH)
    earlier = prior_total[:, None] + jnp.dot(station_loads, strict, precision=HIGH)
    moment_arm = prior_arm[:, None] + jnp.dot(placed_loads, strict, precision=HIGH)
    inv_root = 1.0 / math.sqrt(panels_total)
    shear = (running * inv_root).reshape(variant_dev, load_count, STATIONS)
    moment = ((station_place[None, :] * earlier - moment_arm) * inv_root).reshape(
        variant_dev, load_count, STATIONS
    )
    return (shear, moment)


TILE_ROWS = 8
HALF_ROWS = 4
LANES = 128
LOAD_GRANT = 16 << 20
FUSED_PANELS = 1024


def own_geometry_rows(weights_of, points_col, corner_rows_of, control_ref, vert_dev, before_chunk):
    controls = control_ref.shape[1]
    chunk = min(controls, 2 * LANES)
    totals = [jnp.zeros((vert_dev, chunk), jnp.float32) for _ in range(3)]
    columns = [jnp.broadcast_to(col, (vert_dev, chunk)) for col in points_col]
    for start in range(0, controls, chunk):
        span = slice(start, start + chunk)
        before_chunk(start)
        weights = weights_of(span)
        dx = control_ref[0:1, span] - columns[0]
        dy = control_ref[1:2, span] - columns[1]
        dz = control_ref[2:3, span] - columns[2]
        basis = lax.rsqrt(1.0 + (dx * dx + dy * dy + dz * dz))
        totals = [totals[a] + weights[a] * basis for a in range(3)]
    moved = [points_col[a] + jnp.sum(totals[a], axis=1, keepdims=True) for a in range(3)]
    corner_rows = corner_rows_of()
    vertex = lax.broadcasted_iota(jnp.int32, (vert_dev, corner_rows.shape[1]), 0)
    corners = []
    for q in range(3):
        hit = vertex == corner_rows[q : q + 1, :]
        corners.append(
            [jnp.sum(jnp.where(hit, moved[a], 0.0), axis=0, keepdims=True) for a in range(3)]
        )
    p0, p1, p2 = corners
    centroid = [(p0[a] + p1[a] + p2[a]) / 3.0 for a in range(3)]
    e1 = [p1[a] - p0[a] for a in range(3)]
    e2 = [p2[a] - p0[a] for a in range(3)]
    area = [
        0.5 * (e1[1] * e2[2] - e1[2] * e2[1]),
        0.5 * (e1[2] * e2[0] - e1[0] * e2[2]),
        0.5 * (e1[0] * e2[1] - e1[1] * e2[0]),
    ]
    weight = jnp.sqrt(area[0] * area[0] + area[1] * area[1] + area[2] * area[2] + SKIN_SQUARE)
    return centroid, weight, area


def gather_kernel(
    panels_axis,
    cols_axis,
    order_hbm,
    base_hbm,
    control_hbm,
    morph_hbm,
    corner_hbm,
    flag_hbm,
    owner_hbm,
    velocity_hbm,
    influence_ref,
    masks_ref,
    boundary_ref,
    lift_ref,
    order_ref,
    base_ref,
    control_ref,
    morph_ref,
    corner_ref,
    flag_ref,
    owner_ref,
    velocity_ref,
    mix_ref,
    spread_ref,
    gathered,
    in_sem,
    send_sem,
    recv_sem,
):
    owners = panels_axis * cols_axis
    row, col = lax.axis_index("panels"), lax.axis_index("cols")
    me = row * cols_axis + col
    vert_dev = base_ref.shape[1]
    pan_dev = corner_ref.shape[1]
    loads = velocity_ref.shape[1]
    panels_total = pan_dev * owners

    halves = 2
    wide = control_ref.shape[1] // halves
    pairs = [(base_hbm, base_ref), (order_hbm, order_ref)]
    for half in range(halves):
        span = pl.ds(half * wide, wide)
        pairs += [
            (control_hbm.at[:, span], control_ref.at[:, span]),
            (morph_hbm.at[:, :, span], morph_ref.at[:, :, span]),
        ]
    pairs += [
        (corner_hbm, corner_ref),
        (flag_hbm, flag_ref),
        (owner_hbm, owner_ref),
        (velocity_hbm, velocity_ref),
    ]
    fetches = [
        pltpu.make_async_copy(source, target, in_sem.at[k])
        for k, (source, target) in enumerate(pairs)
    ]
    for fetch in fetches:
        fetch.start()
    steps = [
        (r % panels_axis, c)
        for r in range(1, panels_axis + 1)
        for c in reversed(range(cols_axis))
    ][:-1]
    peers = [
        {"panels": lax.rem(row + r, panels_axis), "cols": lax.rem(col + c, cols_axis)}
        for r, c in steps
    ]
    barrier = pltpu.get_barrier_semaphore()
    for peer in peers:
        pl.semaphore_signal(barrier, inc=1, device_id=peer, device_id_type=pl.DeviceIdType.MESH)
    mix_ref[...] = jnp.zeros(mix_ref.shape, jnp.float32)
    fetches[0].wait()
    mix_ref[0:3, 0:vert_dev] = base_ref[...]
    mixed = mix_ref[...].T
    points_col = [mixed[0:vert_dev, a : a + 1] for a in range(3)]
    fetches[1].wait()
    slot = order_ref[lax.axis_index("phase")]

    def before_chunk(start):
        if start % wide == 0:
            for part in range(2):
                fetches[2 + 2 * (start // wide) + part].wait()

    def weights_of(span):
        picked = [morph_ref[a, 0:1, span] for a in range(3)]
        for v in range(1, morph_ref.shape[1]):
            other = [morph_ref[a, v : v + 1, span] for a in range(3)]
            picked = [jnp.where(slot == v, new, old) for new, old in zip(other, picked)]
        return picked

    def corner_rows_of():
        for fetch in fetches[-4:]:
            fetch.wait()
        return corner_ref[...] - me * vert_dev

    centroid, weight, area = own_geometry_rows(
        weights_of,
        points_col,
        corner_rows_of,
        control_ref,
        vert_dev,
        before_chunk,
    )
    hull = (1 - flag_ref[...]).astype(jnp.float32)
    station = (
        owner_ref[...] * STATIONS
        + lax.rem(me * pan_dev, STATIONS)
        + lax.broadcasted_iota(jnp.int32, (1, pan_dev), 1)
    ).astype(jnp.float32)
    upper = jnp.concatenate(centroid + [weight], axis=0)
    lower = jnp.concatenate([part * hull for part in area] + [station], axis=0)
    gathered[me] = jnp.concatenate([upper, lower], axis=1)

    pl.semaphore_wait(barrier, owners - 1)
    sends = []
    for k, peer in enumerate(peers):
        send = pltpu.make_async_remote_copy(
            src_ref=gathered.at[me],
            dst_ref=gathered.at[me],
            send_sem=send_sem.at[k],
            recv_sem=recv_sem.at[me],
            device_id=peer,
            device_id_type=pl.DeviceIdType.MESH,
        )
        send.start()
        sends.append(send)

    mix_ref[0:3, 0:loads] = velocity_ref[...]
    velocity = mix_ref[...].T
    velocity_col = [velocity[0:loads, a : a + 1] for a in range(3)]
    here = (me * STATIONS + lax.broadcasted_iota(jnp.int32, (LANES, STATIONS), 1)).astype(
        jnp.float32
    )
    kernel_scale = 1.0 / (4.0 * math.pi * math.sqrt(panels_total))
    tiles = panels_total // LANES
    per_tile = owners // tiles
    block = 32

    def influence_of(target_row, source):
        dx = target_row[0:1] - source[0]
        dy = target_row[1:2] - source[1]
        dz = target_row[2:3] - source[2]
        distance = dx * dx + dy * dy + dz * dz
        return (source[3] * lax.rsqrt(distance + CORE_SQUARE)).astype(jnp.bfloat16)

    tile_rows = []
    for tile in range(tiles):
        for source in range(tile * per_tile, (tile + 1) * per_tile):

            @pl.when(me != source)
            def _():
                pltpu.make_async_remote_copy(
                    src_ref=gathered.at[source],
                    dst_ref=gathered.at[source],
                    send_sem=send_sem.at[0],
                    recv_sem=recv_sem.at[source],
                    device_id=peers[0],
                    device_id_type=pl.DeviceIdType.MESH,
                ).wait_recv()

        blocks = [gathered[tile * per_tile + d] for d in range(per_tile)]
        own = jnp.concatenate([part[:, 0:pan_dev] for part in blocks], axis=1)
        load = jnp.concatenate([part[:, pan_dev : 2 * pan_dev] for part in blocks], axis=1)
        tile_rows.append(own)
        columns = jnp.concatenate([own, load], axis=0).T
        lanes = slice(tile * LANES, (tile + 1) * LANES)
        boundary_ref[:, lanes] = (
            velocity_col[0] * load[0:1] + velocity_col[1] * load[1:2] + velocity_col[2] * load[2:3]
        )
        lift_ref[:, lanes] = load[2:3]
        for start in range(0, tile * LANES, block):
            span = slice(start, start + block)
            influence_ref[span, lanes] = influence_of(
                own, [spread_ref[a, span, :] for a in range(4)]
            )
        for a in range(4):
            column = columns[:, a : a + 1] * kernel_scale if a == 3 else columns[:, a : a + 1]
            spread_ref[a, lanes, :] = jnp.broadcast_to(column, (LANES, LANES))
        for start in range(0, LANES, block):
            span = slice(tile * LANES + start, tile * LANES + start + block)
            source = [spread_ref[a, span, :] for a in range(4)]
            for target in range(tile + 1):
                influence_ref[span, target * LANES : (target + 1) * LANES] = influence_of(
                    tile_rows[target], source
                )
        gap = here - columns[:, 7:8]
        arm = jnp.maximum(gap, 0.0)
        arm_high = arm.astype(jnp.bfloat16)
        masks_ref[lanes, 0:STATIONS] = jnp.where(gap >= 0.0, 1.0, 0.0).astype(jnp.bfloat16)
        masks_ref[lanes, STATIONS : 2 * STATIONS] = arm_high
        masks_ref[lanes, 2 * STATIONS :] = (arm - arm_high.astype(jnp.float32)).astype(
            jnp.bfloat16
        )
    for send in sends:
        send.wait_send()


def load_kernel(owners, influence_ref, masks_ref, boundary_ref, lift_ref, shear_ref, moment_ref):
    loads, panels_total = boundary_ref.shape
    boundary = boundary_ref[...]
    first = boundary.astype(jnp.bfloat16)
    induced = jnp.dot(first, influence_ref[...], preferred_element_type=jnp.float32)
    second = (first.astype(jnp.float32) + (boundary - induced)).astype(jnp.bfloat16)
    pressure = jnp.dot(second, influence_ref[...], preferred_element_type=jnp.float32)
    force = pressure * lift_ref[...]
    force_high = force.astype(jnp.bfloat16)
    force_low = (force - force_high.astype(jnp.float32)).astype(jnp.bfloat16)
    summed = jnp.dot(
        jnp.concatenate([force_high, force_low], axis=0),
        masks_ref[...],
        preferred_element_type=jnp.float32,
    )
    summed = summed[0:loads] + summed[loads : 2 * loads]
    inv_root = 1.0 / math.sqrt(panels_total)
    shear_ref[0] = summed[:, 0:STATIONS] * inv_root
    moment_ref[0] = (summed[:, STATIONS : 2 * STATIONS] + summed[:, 2 * STATIONS :]) * (
        inv_root / (STATIONS * owners)
    )


def fused_shards(
    panels_axis,
    cols_axis,
    base_points,
    control_points,
    morph_weights,
    connectivity,
    free_flags,
    station_owner,
    variant_order,
    load_velocity,
):
    owners = panels_axis * cols_axis
    pan_dev = connectivity.shape[1]
    loads = load_velocity.shape[0]
    panels_total = pan_dev * owners
    hbm_inputs = (
        variant_order,
        base_points,
        control_points,
        morph_weights.transpose(1, 0, 2),
        connectivity,
        free_flags.reshape(1, pan_dev),
        station_owner.reshape(1, pan_dev),
        load_velocity.T,
    )
    parts = pl.pallas_call(
        functools.partial(gather_kernel, panels_axis, cols_axis),
        out_shape=(
            pltpu.VMEM((panels_total, panels_total), jnp.bfloat16),
            pltpu.VMEM((panels_total, 3 * STATIONS), jnp.bfloat16),
            pltpu.VMEM((loads, panels_total), jnp.float32),
            pltpu.VMEM((1, panels_total), jnp.float32),
        ),
        in_specs=[pl.BlockSpec(memory_space=pltpu.HBM)] * len(hbm_inputs),
        out_specs=(pl.BlockSpec(memory_space=pltpu.VMEM),) * 4,
        scratch_shapes=[pltpu.SMEM(variant_order.shape, variant_order.dtype)]
        + [pltpu.VMEM(part.shape, part.dtype) for part in hbm_inputs[1:]]
        + [
            pltpu.VMEM((TILE_ROWS, LANES), jnp.float32),
            pltpu.VMEM((HALF_ROWS, panels_total, LANES), jnp.float32),
            pltpu.VMEM((owners, HALF_ROWS, LANES), jnp.float32),
            pltpu.SemaphoreType.DMA((len(hbm_inputs) + 2,)),
            pltpu.SemaphoreType.DMA((owners,)),
            pltpu.SemaphoreType.DMA((owners,)),
        ],
        compiler_params=pltpu.CompilerParams(
            collective_id=0, has_side_effects=True
        ),
    )(*hbm_inputs)
    result = jax.ShapeDtypeStruct((1, loads, STATIONS), jnp.float32)
    return tuple(
        pl.pallas_call(
            functools.partial(load_kernel, owners),
            out_shape=(result, result),
            in_specs=[pl.BlockSpec(memory_space=pltpu.VMEM)] * 4,
            out_specs=(pl.BlockSpec(memory_space=pltpu.VMEM),) * 2,
            compiler_params=pltpu.CompilerParams(vmem_limit_bytes=LOAD_GRANT),
        )(*parts)
    )


def choose_shards(mesh, *arrays):
    panels_axis, cols_axis = mesh.shape["panels"], mesh.shape["cols"]
    owners = panels_axis * cols_axis
    base_points, connectivity, variant_order, load_velocity = (
        arrays[0],
        arrays[3],
        arrays[6],
        arrays[7],
    )
    pan_dev = connectivity.shape[1]
    fits = (
        pan_dev * owners <= FUSED_PANELS
        and LANES == 2 * pan_dev
        and STATIONS % pan_dev == 0
        and owners % 2 == 0
        and base_points.shape[1] <= LANES
        and load_velocity.shape[0] <= LANES
        and variant_order.shape[0] == mesh.shape["phase"]
    )
    if fits:
        return fused_shards(panels_axis, cols_axis, *arrays)
    return shards(*arrays)


def solution(mesh):
    return jax.shard_map(
        functools.partial(choose_shards, mesh),
        mesh=mesh,
        in_specs=(
            P(None, ("groups", "panels", "cols")),
            P(),
            P("groups", None, None),
            P(None, ("groups", "panels", "cols")),
            P(("groups", "panels", "cols")),
            P(("groups", "panels", "cols"), None),
            P("groups"),
            P(),
        ),
        out_specs=(
            P(("groups", "phase"), None, ("panels", "cols")),
            P(("groups", "phase"), None, ("panels", "cols")),
        ),
        check_vma=False,
    )
```
